32 devices in a mesh: group: 2 (over y), rows: 4 (over z), sec: 2 (over x), sub: 2 (over core).
Axes of the slice: x: 2, y: 2, z: 4, core: 2. Of those that a mesh axis runs over, the one named last changes fastest.
Arguments:
- row_seeds: int32 [16384], P(('group', 'rows')), parts along dimension 0, may hold values from 0 to 65520
- labels: int32 [16384], P(('group', 'rows')), parts along dimension 0, may hold values from 0 to 1
- weights: float32 [131072], P(('group', 'sec', 'sub')), parts along dimension 0, may hold values from -5 to 5
- sketch: bfloat16 [65536, 64], P(('sec', 'sub')), may hold values from -5 to 5
Outputs:
- step: float32 [131072], P(('group', 'sec', 'sub')), parts along dimension 0
- sketched: float32 [131072, 64], P(('group', 'sec', 'sub')), parts along dimension 0
The draws below stay inside these ranges and needn't reach their ends.
There are 2 independent parts, one for each index of `group`. The reference program is written for one: setup_inputs(seed, part) draws one part's arguments, and reference() takes and returns one part's arrays. A program takes and returns all parts, laid end to end along the dimension named above; an argument that names none is the same for every part. Nothing has to cross between parts.
All inputs are finite; a program needn't handle non-finite values.
Results may differ from the reference program's by a relative error of at most 0.0029.
Values may be sent and summed in bfloat16 or wider, within the bound.
No kernel may reach another device: no remote copies, remote signals or barrier semaphores. Data moves between devices by JAX's collectives and lax.ppermute only.
A program may use at most 128 MiB of HBM per device.

```python
import jax
import jax.numpy as jnp
from jax import lax

FEAT = 65536
ROOT = 256
RANK = 64
NROWS = 8192


def plant(entries, rng, smallest, high):
    extent = entries.shape
    index_at = [jax.random.randint(jax.random.fold_in(rng, axis), (), 0, extent[axis]) for axis in range(len(extent))]
    entries = entries.at[tuple(index_at)].set(smallest)
    longest = extent.index(max(extent))
    index_at[longest] = (index_at[longest] + 1) % extent[longest]
    return entries.at[tuple(index_at)].set(high)


def steps_of(key, shape, pieces, low, largest):
    factor_of, own = 1.0, jax.random.fold_in(key, 6)
    for position, shards_of in pieces:
        draws = jnp.exp(jax.random.uniform(jax.random.fold_in(own, position), (shards_of,), jnp.float32, low / len(pieces), largest / len(pieces)))
        factor_of = factor_of * jnp.repeat(draws, shape[position] // shards_of).reshape([-1 if axis == position else 1 for axis in range(len(shape))])
    return factor_of


def scatter_about(own_key, extent, width, bound, split=(), dtype=jnp.bfloat16):
    array = jax.random.normal(own_key, extent, jnp.float32) * width
    if len(split) > 0:
        array = steps_of(own_key, extent, split, -0.22, 0.18) * array
    return jnp.clip(array, min=-bound, max=bound).astype(dtype)


def setup_inputs(seed: int = 0, part: int = 0) -> dict:
    key_of = jax.random.split(jax.random.key(seed), 5)
    own_keys = jax.random.split(jax.random.fold_in(key_of[4], part), 5)
    row_seeds = plant(jax.random.randint(own_keys[0], (NROWS,), 0, 65521), jax.random.fold_in(own_keys[0], 1), 0, 65520).astype(jnp.int32)
    labels = plant(jax.random.randint(own_keys[1], (NROWS,), 0, 2), jax.random.fold_in(own_keys[1], 1), 0, 1).astype(jnp.int32)
    weights = scatter_about(own_keys[2], (FEAT,), 1.0, 5.0, ((0, 4),), jnp.float32)
    sketch = scatter_about(key_of[3], (FEAT, RANK), 1.0, 5.0, ((0, 4),))
    return dict(row_seeds=row_seeds, labels=labels, weights=weights, sketch=sketch)


def table_block(seeds, first, count):
    cols = first + lax.iota(jnp.int32, count)
    part_a = cols * 30011 % 65521
    part_b = seeds * 16411 % 65521
    mixer = (part_b[:, None] + part_a[None, :]) % 65521
    folded = mixer % 46337
    mixer = folded * folded % 65521
    mixer = (mixer * 31 + part_a[None, :] + 7) % 65521
    level = mixer % 16
    return ((level.astype(jnp.float32) - 7.5) * (1.0 / (4.0 * ROOT))).astype(jnp.bfloat16)

def reference(row_seeds, labels, weights, sketch):
    lam = 0.05
    total_rows = row_seeds.shape[0]
    nfeat = weights.shape[0]
    blk = 256 if total_rows % 256 == 0 else total_rows
    nblk = total_rows // blk
    stacked = jnp.concatenate([weights.astype(jnp.bfloat16)[:, None], sketch], axis=1)
    seed_blocks = row_seeds.reshape(nblk, blk)

    def margin_block(seeds):
        return jnp.dot(table_block(seeds, 0, nfeat).astype(jnp.float32), stacked.astype(jnp.float32), preferred_element_type=jnp.float32)
    margins = lax.map(margin_block, seed_blocks).reshape(total_rows, stacked.shape[1])
    prob = jax.nn.sigmoid(margins[:, 0])
    resid = prob - labels.astype(jnp.float32)
    curv = prob * (1.0 - prob)
    mixed = jnp.concatenate([resid[:, None], curv[:, None] * margins[:, 1:]], axis=1).astype(jnp.bfloat16)
    mixed_blocks = mixed.reshape(nblk, blk, mixed.shape[1])

    def add_block(acc, pair):
        seeds, rows_mixed = pair
        tab = table_block(seeds, 0, nfeat)
        return (acc + lax.dot_general(tab.astype(jnp.float32), rows_mixed.astype(jnp.float32), (((0,), (0,)), ((), ())), preferred_element_type=jnp.float32), None)
    total, _ = lax.scan(add_block, jnp.zeros((nfeat, mixed.shape[1]), jnp.float32), (seed_blocks, mixed_blocks))
    grad = total[:, 0] + lam * weights
    sketched = total[:, 1:] + lam * sketch.astype(jnp.float32)
    highest = lax.Precision.HIGHEST
    core = lax.dot_general(sketch.astype(jnp.float32), sketched, (((0,), (0,)), ((), ())), precision=highest)
    square = lax.dot_general(sketched, sketched, (((0,), (0,)), ((), ())), precision=highest)
    proj = lax.dot_general(sketched, grad, (((0,), (0,)), ((), ())), precision=highest)
    inner = lam * core + square
    inner = 0.5 * (inner + inner.T)
    factor = jnp.linalg.cholesky(inner)
    middle = lax.linalg.triangular_solve(factor, proj[:, None], left_side=True, lower=True)
    coef = lax.linalg.triangular_solve(factor, middle, left_side=True, lower=True, transpose_a=True)[:, 0]
    step = (grad - jnp.dot(sketched, coef, precision=highest)) / lam
    return (step, sketched)
```

```python
import functools

import jax
import jax.numpy as jnp
from jax import lax
from jax.experimental import pallas as pl
from jax.experimental.pallas import tpu as pltpu
from jax.sharding import PartitionSpec as P

PRIME = 65521
FOLD = 46337
STEP_A = 30011
STEP_B = 16411
SHIFT = STEP_B * pow(STEP_A, -1, PRIME) % PRIME
LAM = 0.05
SCALE = 1.0 / 1024.0
LANES = 128


def window_table(length):
    rows = -(-length // (8 * LANES)) * 8
    n = lax.broadcasted_iota(jnp.int32, (rows, LANES), 0) * LANES + lax.broadcasted_iota(
        jnp.int32, (rows, LANES), 1
    )
    mixer = n % PRIME * STEP_A % PRIME
    folded = mixer % FOLD
    entry = (folded * folded % PRIME * 31 + 7) % PRIME
    return entry.astype(jnp.float32) - (PRIME - 0.5)


def window_starts(seeds, first):
    high = seeds * (SHIFT // 256) % PRIME
    return (high * 256 + seeds * (SHIFT % 256) + first) % PRIME


def table_body(start_ref, tab_ref, a_ref, feat_ref, data_ref, marg_ref, scr, *, unroll, pitch):
    nrow, nfeat = data_ref.shape
    nsub = nfeat // LANES
    high = min(8, nsub)
    lane = lax.broadcasted_iota(jnp.int32, (high, LANES), 1)
    base = pl.program_id(0) * nrow
    part = a_ref[...]

    def samples(group, carry):
        for u in range(unroll):
            row = group * unroll + u
            start = start_ref[base + row]
            top = start >> 7
            off = start & (LANES - 1)
            early = lane < off
            one = tab_ref[pl.ds(top, nsub), :]
            two = tab_ref[pl.ds(top + 1, nsub), :]
            for v in range(0, nsub, high):
                win = jnp.where(early, two[v : v + high], one[v : v + high])
                win = pltpu.roll(win, LANES - off, 1)
                level = (win + part[v : v + high]).astype(jnp.int32) & 15
                scr[pl.ds(row + v * pitch, high, stride=pitch), :] = level.astype(jnp.float32)
        return carry

    lax.fori_loop(0, nrow // unroll, samples, 0)
    for r in range(nsub):
        data_ref[:, r * LANES : (r + 1) * LANES] = scr[pl.ds(r * pitch, nrow), :].astype(jnp.bfloat16)
    marg_ref[...] = lax.dot_general(
        feat_ref[...], data_ref[...], (((1,), (1,)), ((), ())), preferred_element_type=jnp.float32
    )


def make_table(starts, tab, part, feats):
    count = starts.shape[0]
    nsub = part.shape[0]
    nfeat = nsub * LANES
    ncol = feats.shape[0]
    nrow = min(256, count)
    pitch = nrow + 8
    return pl.pallas_call(
        functools.partial(table_body, unroll=64, pitch=pitch),
        grid_spec=pltpu.PrefetchScalarGridSpec(
            num_scalar_prefetch=1,
            grid=(count // nrow,),
            in_specs=[
                pl.BlockSpec(tab.shape, lambda i, s: (0, 0)),
                pl.BlockSpec(part.shape, lambda i, s: (0, 0)),
                pl.BlockSpec((ncol, nfeat), lambda i, s: (0, 0)),
            ],
            out_specs=[
                pl.BlockSpec((nrow, nfeat), lambda i, s: (i, 0)),
                pl.BlockSpec((ncol, nrow), lambda i, s: (0, i)),
            ],
            scratch_shapes=[pltpu.VMEM((nsub * pitch, LANES), jnp.float32)],
        ),
        out_shape=[
            jax.ShapeDtypeStruct((count, nfeat), jnp.bfloat16),
            jax.ShapeDtypeStruct((ncol, count), jnp.float32),
        ],
        compiler_params=pltpu.CompilerParams(vmem_limit_bytes=48 << 20),
        cost_estimate=pl.CostEstimate(
            flops=count * nfeat * 1500, bytes_accessed=count * nfeat * 2, transcendentals=0
        ),
        name="make_table",
    )(starts, tab, part, feats)


def back_body(mix_ref, data_ref, old_ref, out_ref):
    @pl.when(pl.program_id(1) == 0)
    def _():
        out_ref[...] = old_ref[...]

    out_ref[...] += jnp.dot(mix_ref[...], data_ref[...], preferred_element_type=jnp.float32)


def back(mixed, data, total):
    ncol, count = mixed.shape
    nfeat = data.shape[1]
    kb = min(1024, count)
    fb = min(4096, nfeat)
    return pl.pallas_call(
        back_body,
        grid=(nfeat // fb, count // kb),
        in_specs=[
            pl.BlockSpec((ncol, kb), lambda f, k: (0, k)),
            pl.BlockSpec((kb, fb), lambda f, k: (k, f)),
            pl.BlockSpec((ncol, fb), lambda f, k: (0, f)),
        ],
        out_specs=pl.BlockSpec((ncol, fb), lambda f, k: (0, f)),
        out_shape=jax.ShapeDtypeStruct((ncol, nfeat), jnp.float32),
        compiler_params=pltpu.CompilerParams(vmem_limit_bytes=48 << 20),
        cost_estimate=pl.CostEstimate(
            flops=2 * count * nfeat * ncol, bytes_accessed=count * nfeat * 2, transcendentals=0
        ),
        name="back",
    )(mixed, data, total)


def shift(x, axis, size, by):
    return lax.ppermute(x, axis, [(i, (i + by) % size) for i in range(size)])


def scatter_sum(x, axis, size):
    if size <= 4:
        total = x[:, 0]
        for d in range(1, size):
            total = total + shift(x[:, d], axis, size, d)
        return total

    def hop(i, acc):
        return shift(acc, axis, size, 1) + lax.dynamic_index_in_dim(x, size - 2 - i, 1, False)

    return lax.fori_loop(0, size - 1, hop, x[:, size - 1])


def collect(x, axis, size, at):
    if size <= 4:
        return jnp.stack([x] + [shift(x, axis, size, -d) for d in range(1, size)], axis=at)

    def hop(cur, _):
        cur = shift(cur, axis, size, -1)
        return cur, cur

    _, rest = lax.scan(hop, x, None, length=size - 1)
    return jnp.moveaxis(jnp.concatenate([x[None], rest], axis=0), 0, at)


def all_sum(x, axis, size):
    if size & (size - 1) == 0 and size <= 4:
        step = 1
        while step < size:
            x = x + lax.ppermute(x, axis, [(i, i ^ step) for i in range(size)])
            step *= 2
        return x
    return lax.psum(x, axis)


def roll_to(x, dim, size, index):
    return lax.dynamic_slice_in_dim(jnp.concatenate([x, x], axis=dim), index, size, dim)


def weigh(margins, labels):
    prob = jax.nn.sigmoid(margins[64:])
    resid = prob - labels.astype(jnp.float32)
    return jnp.concatenate([prob * (1.0 - prob) * margins[:64], resid], axis=0).astype(jnp.bfloat16)


def local(sizes, row_seeds, labels, weights, sketch):
    nrows, nsec, nsub = sizes
    count = row_seeds.shape[0]
    rank = sketch.shape[1]
    nfeat = weights.shape[0] // nrows
    z, s, u = lax.axis_index("rows"), lax.axis_index("sec"), lax.axis_index("sub")
    own = z * nfeat
    first = (s * nsub + u) * weights.shape[0] + own

    nchunk = 4
    piece = count // (nchunk * nsec * nsub)
    seeds = row_seeds.reshape(nchunk, nsec, nsub, piece)
    seeds = roll_to(roll_to(seeds, 1, nsec, s), 2, nsub, u)
    starts = window_starts(collect(seeds, "rows", nrows, 3).transpose(0, 2, 1, 3, 4), first)
    starts = starts.reshape(nchunk, -1)
    labels = labels.reshape(nchunk, nsec, nsub, piece)
    labels = lax.dynamic_slice(labels, (0, s, u, 0), (nchunk, 1, 1, piece)).reshape(nchunk, 1, piece)

    tab = window_table(PRIME + nfeat + LANES)
    cols = first + lax.iota(jnp.int32, nfeat)
    part = (cols * STEP_A % PRIME).astype(jnp.float32).reshape(nfeat // LANES, LANES)
    sketch_t = lax.dynamic_slice_in_dim(sketch.T, own, nfeat, 1)
    own_weights = lax.dynamic_slice_in_dim(weights, own, nfeat, 0)[None]
    feats = jnp.concatenate([sketch_t, own_weights.astype(jnp.bfloat16)], axis=0)
    ncol = rank + 1
    feat_sum = jnp.sum(feats.astype(jnp.float32), axis=1, keepdims=True) * 7.5

    datas, mixes = [], []
    for c in range(nchunk):
        data, marg = make_table(starts[c], tab, part, feats)
        marg = (marg - feat_sum) * SCALE
        marg = scatter_sum(marg.reshape(ncol, nsub, -1), "sub", nsub)
        marg = scatter_sum(marg.reshape(ncol, nsec, -1), "sec", nsec)
        marg = scatter_sum(marg.reshape(ncol, nrows, -1), "rows", nrows)
        mixed = weigh(marg, labels[c])
        mixed = collect(mixed, "rows", nrows, 1).reshape(ncol, -1)
        mixed = collect(mixed, "sec", nsec, 1).reshape(ncol, -1)
        mixed = collect(mixed, "sub", nsub, 1).reshape(ncol, -1)
        datas.append(data)
        mixes.append(mixed)

    total = jnp.zeros((ncol, nfeat), jnp.float32)
    mix_sum = 0.0
    for data, mixed in zip(datas, mixes):
        total = back(mixed, data, total)
        mix_sum = mix_sum + jnp.sum(mixed.astype(jnp.float32), axis=1, keepdims=True)
    total = (total - 7.5 * mix_sum) * SCALE

    sketch_f = sketch_t.astype(jnp.float32)
    grad = total[rank:] + LAM * own_weights
    sketched = total[:rank] + LAM * sketch_f
    left = jnp.concatenate([LAM * sketch_f + sketched, grad], axis=0)
    prods = lax.dot_general(
        left, sketched, (((1,), (1,)), ((), ())), precision=lax.Precision.HIGHEST
    )
    prods = all_sum(all_sum(all_sum(prods, "sub", nsub), "sec", nsec), "rows", nrows)
    inner = prods[:rank]
    inner = 0.5 * (inner + inner.T)
    factor = jnp.linalg.cholesky(inner)
    middle = lax.linalg.triangular_solve(factor, prods[rank:].T, left_side=True, lower=True)
    coef = lax.linalg.triangular_solve(
        factor, middle, left_side=True, lower=True, transpose_a=True
    )
    step = (grad - jnp.dot(coef.T, sketched, precision=lax.Precision.HIGHEST)) / LAM

    def spread(x):
        parts = collect(x, "rows", nrows, 0)
        parts = roll_to(parts, 0, nrows, (nrows - z) % nrows)
        return jnp.moveaxis(parts, 0, 1).reshape(x.shape[0], -1).astype(jnp.float32)

    wide = spread(sketched.astype(jnp.bfloat16))
    return (spread(step)[0], wide.T)


def solution(mesh):
    placed = (
        P(("group", "rows")),
        P(("group", "rows")),
        P(("group", "sec", "sub")),
        P(("sec", "sub"), None),
    )
    sizes = tuple(mesh.shape[name] for name in ("rows", "sec", "sub"))
    return jax.shard_map(
        functools.partial(local, sizes),
        mesh=mesh,
        in_specs=placed,
        out_specs=(P(("group", "sec", "sub")), P(("group", "sec", "sub"), None)),
        check_vma=False,
    )
```

```python
import functools

import jax
import jax.numpy as jnp
from jax import lax
from jax.experimental import pallas as pl
from jax.experimental.pallas import tpu as pltpu
from jax.sharding import PartitionSpec as P

PRIME = 65521
FOLD = 46337
STEP_A = 30011
STEP_B = 16411
SHIFT = STEP_B * pow(STEP_A, -1, PRIME) % PRIME
LAM = 0.05
SCALE = 1.0 / 1024.0
LANES = 128


def window_table(length):
    rows = -(-length // (8 * LANES)) * 8
    n = lax.broadcasted_iota(jnp.int32, (rows, LANES), 0) * LANES + lax.broadcasted_iota(
        jnp.int32, (rows, LANES), 1
    )
    mixer = n % PRIME * STEP_A % PRIME
    folded = mixer % FOLD
    entry = (folded * folded % PRIME * 31 + 7) % PRIME
    return entry.astype(jnp.float32) - (PRIME - 0.5)


def window_starts(seeds, first):
    high = seeds * (SHIFT // 256) % PRIME
    return (high * 256 + seeds * (SHIFT % 256) + first) % PRIME


def table_body(start_ref, tab_ref, a_ref, feat_ref, data_ref, marg_ref, scr, *, unroll, pitch):
    nrow, nfeat = data_ref.shape
    nsub = nfeat // LANES
    high = min(8, nsub)
    lane = lax.broadcasted_iota(jnp.int32, (high, LANES), 1)
    base = pl.program_id(0) * nrow
    part = a_ref[...]

    def samples(group, carry):
        for u in range(unroll):
            row = group * unroll + u
            start = start_ref[base + row]
            top = start >> 7
            off = start & (LANES - 1)
            early = lane < off
            one = tab_ref[pl.ds(top, nsub), :]
            two = tab_ref[pl.ds(top + 1, nsub), :]
            for v in range(0, nsub, high):
                win = jnp.where(early, two[v : v + high], one[v : v + high])
                win = pltpu.roll(win, LANES - off, 1)
                level = (win + part[v : v + high]).astype(jnp.int32) & 15
                scr[pl.ds(row + v * pitch, high, stride=pitch), :] = level.astype(jnp.float32) - 7.5
        return carry

    lax.fori_loop(0, nrow // unroll, samples, 0)
    for r in range(nsub):
        data_ref[:, r * LANES : (r + 1) * LANES] = scr[pl.ds(r * pitch, nrow), :].astype(jnp.bfloat16)
    marg_ref[...] = SCALE * lax.dot_general(
        feat_ref[...], data_ref[...], (((1,), (1,)), ((), ())), preferred_element_type=jnp.float32
    )


def make_table(starts, tab, part, feats):
    count = starts.shape[0]
    nsub = part.shape[0]
    nfeat = nsub * LANES
    ncol = feats.shape[0]
    nrow = min(256, count)
    pitch = nrow + 8
    return pl.pallas_call(
        functools.partial(table_body, unroll=64, pitch=pitch),
        grid_spec=pltpu.PrefetchScalarGridSpec(
            num_scalar_prefetch=1,
            grid=(count // nrow,),
            in_specs=[
                pl.BlockSpec(tab.shape, lambda i, s: (0, 0)),
                pl.BlockSpec(part.shape, lambda i, s: (0, 0)),
                pl.BlockSpec((ncol, nfeat), lambda i, s: (0, 0)),
            ],
            out_specs=[
                pl.BlockSpec((nrow, nfeat), lambda i, s: (i, 0)),
                pl.BlockSpec((ncol, nrow), lambda i, s: (0, i)),
            ],
            scratch_shapes=[pltpu.VMEM((nsub * pitch, LANES), jnp.float32)],
        ),
        out_shape=[
            jax.ShapeDtypeStruct((count, nfeat), jnp.bfloat16),
            jax.ShapeDtypeStruct((ncol, count), jnp.float32),
        ],
        compiler_params=pltpu.CompilerParams(vmem_limit_bytes=48 << 20),
        cost_estimate=pl.CostEstimate(
            flops=count * nfeat * 1500, bytes_accessed=count * nfeat * 2, transcendentals=0
        ),
        name="make_table",
    )(starts, tab, part, feats)


def back_body(mix_ref, data_ref, old_ref, out_ref):
    @pl.when(pl.program_id(1) == 0)
    def _():
        out_ref[...] = old_ref[...]

    out_ref[...] += jnp.dot(mix_ref[...], data_ref[...], preferred_element_type=jnp.float32)


def back(mixed, data, total):
    ncol, count = mixed.shape
    nfeat = data.shape[1]
    kb = min(1024, count)
    fb = min(4096, nfeat)
    return pl.pallas_call(
        back_body,
        grid=(nfeat // fb, count // kb),
        in_specs=[
            pl.BlockSpec((ncol, kb), lambda f, k: (0, k)),
            pl.BlockSpec((kb, fb), lambda f, k: (k, f)),
            pl.BlockSpec((ncol, fb), lambda f, k: (0, f)),
        ],
        out_specs=pl.BlockSpec((ncol, fb), lambda f, k: (0, f)),
        out_shape=jax.ShapeDtypeStruct((ncol, nfeat), jnp.float32),
        compiler_params=pltpu.CompilerParams(vmem_limit_bytes=48 << 20),
        cost_estimate=pl.CostEstimate(
            flops=2 * count * nfeat * ncol, bytes_accessed=count * nfeat * 2, transcendentals=0
        ),
        name="back",
    )(mixed, data, total)


def shift(x, axis, size, by):
    return lax.ppermute(x, axis, [(i, (i + by) % size) for i in range(size)])


def scatter_sum(x, axis, size):
    if size <= 4:
        total = x[:, 0]
        for d in range(1, size):
            total = total + shift(x[:, d], axis, size, d)
        return total

    def hop(i, acc):
        return shift(acc, axis, size, 1) + lax.dynamic_index_in_dim(x, size - 2 - i, 1, False)

    return lax.fori_loop(0, size - 1, hop, x[:, size - 1])


def collect(x, axis, size, at):
    if size <= 4:
        return jnp.stack([x] + [shift(x, axis, size, -d) for d in range(1, size)], axis=at)

    def hop(cur, _):
        cur = shift(cur, axis, size, -1)
        return cur, cur

    _, rest = lax.scan(hop, x, None, length=size - 1)
    return jnp.moveaxis(jnp.concatenate([x[None], rest], axis=0), 0, at)


def all_sum(x, axis, size):
    if size & (size - 1) == 0 and size <= 4:
        step = 1
        while step < size:
            x = x + lax.ppermute(x, axis, [(i, i ^ step) for i in range(size)])
            step *= 2
        return x
    return lax.psum(x, axis)


def roll_to(x, dim, size, index):
    return lax.dynamic_slice_in_dim(jnp.concatenate([x, x], axis=dim), index, size, dim)


def weigh(margins, labels):
    prob = jax.nn.sigmoid(margins[-1:])
    resid = prob - labels.astype(jnp.float32)
    return jnp.concatenate([prob * (1.0 - prob) * margins[:-1], resid], axis=0).astype(jnp.bfloat16)


def after(x, *deps):
    return lax.optimization_barrier((x, *deps))[0]


def split(x, size, at):
    width = x.shape[1] // size
    return x[:, at * width : (at + 1) * width]


def scatter_rows(x, size):
    if size <= 4:
        return split(x, size, 0), [shift(split(x, size, d), "rows", size, d) for d in range(1, size)]
    return scatter_sum(x.reshape(x.shape[0], size, -1), "rows", size), []


def collect_rows(x, size):
    if size <= 4:
        return [x] + [shift(x, "rows", size, -d) for d in range(1, size)]
    return [collect(x, "rows", size, 1).reshape(x.shape[0], -1)]


def local(sizes, row_seeds, labels, weights, sketch):
    nrows, nsec, nsub = sizes
    count = row_seeds.shape[0]
    rank = sketch.shape[1]
    nfeat = weights.shape[0] // nrows
    z, s, u = lax.axis_index("rows"), lax.axis_index("sec"), lax.axis_index("sub")
    own = z * nfeat
    first = (s * nsub + u) * weights.shape[0] + own

    nchunk = 2
    piece = count // (nchunk * nsec * nsub)
    seeds = row_seeds.reshape(nchunk, nsec, nsub, piece)
    seeds = roll_to(roll_to(seeds, 1, nsec, s), 2, nsub, u)
    starts = window_starts(collect(seeds, "rows", nrows, 3), first)
    labels = labels.reshape(nchunk, nsec, nsub, piece)
    labels = lax.dynamic_slice(labels, (0, s, u, 0), (nchunk, 1, 1, piece)).reshape(nchunk, 1, piece)

    tab = window_table(PRIME + nfeat + LANES)
    cols = first + lax.iota(jnp.int32, nfeat)
    part = (cols * STEP_A % PRIME).astype(jnp.float32).reshape(nfeat // LANES, LANES)
    sketch_t = lax.dynamic_slice_in_dim(sketch.T, own, nfeat, 1)
    own_weights = lax.dynamic_slice_in_dim(weights, own, nfeat, 0)[None]
    feats = jnp.concatenate([sketch_t, own_weights.astype(jnp.bfloat16)], axis=0)
    ncol = rank + 1

    order = [(c, du, ds) for c in range(nchunk) for du in reversed(range(nsub)) for ds in reversed(range(nsec))]
    data, marg, from_sub, from_sec, mixed, stage = {}, {}, {}, {}, {}, {}
    older, due = [], []

    def advance(c, at, *deps):
        if at == 0:
            held, come = scatter_rows(sum(from_sec[c][1:], from_sec[c][0]), nrows)
            stage[c] = (held, come)
            return come or [held]
        if at == 1:
            held, come = stage[c]
            held = after(weigh(sum(come, held), labels[c]), *deps)
            stage[c] = collect_rows(held, nrows)
            return stage[c]
        if at == 2:
            mixed[c, 0, 0] = after(jnp.concatenate(stage[c], axis=1), *deps)
            for ds in range(1, nsec):
                mixed[c, 0, ds] = shift(mixed[c, 0, 0], "sec", nsec, -ds)
            return [mixed[c, 0, ds] for ds in range(1, nsec)]
        if at == 3:
            half = jnp.concatenate([mixed[c, 0, ds] for ds in range(nsec)], axis=1)
            half = after(half, *deps)
            for du in range(1, nsub):
                come = shift(half, "sub", nsub, -du)
                for ds in range(nsec):
                    mixed[c, du, ds] = split(come, nsec, ds)
            return [mixed[c, nsub - 1, 0]]
        return []

    running = []

    def boundary(*deps):
        out = []
        for chunk in list(running):
            out += advance(chunk[0], chunk[1], *deps)
            chunk[1] += 1
            if chunk[1] > 3:
                running.remove(chunk)
        return out

    last = []
    for c, du, ds in order:
        begin = after(starts[c, ds, du].reshape(-1), *last, *older)
        data[c, du, ds], marg[c, du, ds] = make_table(begin, tab, part, feats)
        last = [marg[c, du, ds]]
        older, due = due, boundary()
        if du:
            from_sub[c, du, ds] = shift(marg[c, du, ds], "sub", nsub, du)
            due.append(from_sub[c, du, ds])
        else:
            summed = sum([from_sub[c, e, ds] for e in range(1, nsub)], marg[c, du, ds])
            if ds:
                from_sec.setdefault(c, []).append(shift(summed, "sec", nsec, ds))
                due.append(from_sec[c][-1])
            else:
                from_sec[c].insert(0, summed)
                running.append([c, 0])
                if (c, du, ds) == order[-1]:
                    due += boundary()

    total = jnp.zeros((ncol, nfeat), jnp.float32)
    for c in range(nchunk):
        for du in range(nsub):
            for ds in range(nsec):
                while (c, du, ds) not in mixed:
                    due += boundary()
                total = back(after(mixed[c, du, ds], *older), data[c, du, ds], total)
                older, due = due, boundary(total)
    total = total * SCALE

    sketch_f = sketch_t.astype(jnp.float32)
    grad = total[rank:] + LAM * own_weights
    sketched = total[:rank] + LAM * sketch_f
    block = sketched.astype(jnp.bfloat16)
    wide = {d: shift(block, "rows", nrows, -d) for d in range(1, nrows)} if nrows <= 4 else None
    left = jnp.concatenate([LAM * sketch_f + sketched, grad], axis=0)
    prods = lax.dot_general(
        left, sketched, (((1,), (1,)), ((), ())), precision=lax.Precision.HIGHEST
    )
    prods = all_sum(all_sum(all_sum(prods, "sub", nsub), "sec", nsec), "rows", nrows)
    if wide:
        prods = after(prods, *[wide[d] for d in (1, nrows - 1)])
    inner = prods[:rank]
    inner = 0.5 * (inner + inner.T)
    factor = jnp.linalg.cholesky(inner)
    middle = lax.linalg.triangular_solve(factor, prods[rank:].T, left_side=True, lower=True)
    coef = lax.linalg.triangular_solve(
        factor, middle, left_side=True, lower=True, transpose_a=True
    )
    step = (grad - jnp.dot(coef.T, sketched, precision=lax.Precision.HIGHEST)) / LAM

    def spread(x, rest=None):
        parts = collect(x, "rows", nrows, 0) if rest is None else jnp.stack([x] + rest, axis=0)
        parts = roll_to(parts, 0, nrows, (nrows - z) % nrows)
        return jnp.moveaxis(parts, 0, 1).reshape(x.shape[0], -1).astype(jnp.float32)

    return (spread(step)[0], spread(block, wide and [wide[d] for d in range(1, nrows)]).T)


def solution(mesh):
    placed = (
        P(("group", "rows")),
        P(("group", "rows")),
        P(("group", "sec", "sub")),
        P(("sec", "sub"), None),
    )
    sizes = tuple(mesh.shape[name] for name in ("rows", "sec", "sub"))
    return jax.shard_map(
        functools.partial(local, sizes),
        mesh=mesh,
        in_specs=placed,
        out_specs=(P(("group", "sec", "sub")), P(("group", "sec", "sub"), None)),
        check_vma=False,
    )
```

```python
import functools

import jax
import jax.numpy as jnp
from jax import lax
from jax.experimental import pallas as pl
from jax.experimental.pallas import tpu as pltpu
from jax.sharding import PartitionSpec as P

PRIME = 65521
FOLD = 46337
STEP_A = 30011
STEP_B = 16411
SHIFT = STEP_B * pow(STEP_A, -1, PRIME) % PRIME
LAM = 0.05
SCALE = 1.0 / 1024.0
LANES = 128


def window_table(length):
    rows = -(-length // (8 * LANES)) * 8
    n = lax.broadcasted_iota(jnp.int32, (rows, LANES), 0) * LANES + lax.broadcasted_iota(
        jnp.int32, (rows, LANES), 1
    )
    mixer = n % PRIME * STEP_A % PRIME
    folded = mixer % FOLD
    entry = (folded * folded % PRIME * 31 + 7) % PRIME
    return entry.astype(jnp.float32) - (PRIME - 0.5)


def window_starts(seeds, first):
    high = seeds * (SHIFT // 256) % PRIME
    return (high * 256 + seeds * (SHIFT % 256) + first) % PRIME


def table_body(start_ref, tab_ref, a_ref, feat_ref, data_ref, marg_ref, scr, *, unroll, pitch):
    nrow, nfeat = data_ref.shape
    nsub = nfeat // LANES
    high = min(8, nsub)
    lane = lax.broadcasted_iota(jnp.int32, (high, LANES), 1)
    base = pl.program_id(0) * nrow
    part = a_ref[...]

    def samples(group, carry):
        for u in range(unroll):
            row = group * unroll + u
            start = start_ref[base + row]
            top = start >> 7
            off = start & (LANES - 1)
            early = lane < off
            one = tab_ref[pl.ds(top, nsub), :]
            two = tab_ref[pl.ds(top + 1, nsub), :]
            for v in range(0, nsub, high):
                win = jnp.where(early, two[v : v + high], one[v : v + high])
                win = pltpu.roll(win, LANES - off, 1)
                level = (win + part[v : v + high]).astype(jnp.int32) & 15
                scr[pl.ds(row + v * pitch, high, stride=pitch), :] = level.astype(jnp.float32) - 7.5
        return carry

    lax.fori_loop(0, nrow // unroll, samples, 0)
    for r in range(nsub):
        data_ref[:, r * LANES : (r + 1) * LANES] = scr[pl.ds(r * pitch, nrow), :].astype(jnp.bfloat16)
    marg = lax.dot_general(
        data_ref[...], feat_ref[...], (((1,), (1,)), ((), ())), preferred_element_type=jnp.float32
    )
    marg_ref[...] = SCALE * marg.T[: marg_ref.shape[0]]


def make_table(starts, tab, part, feats, ncol):
    count = starts.shape[0]
    nsub = part.shape[0]
    nfeat = nsub * LANES
    nrow = min(256, count)
    pitch = nrow + 8
    return pl.pallas_call(
        functools.partial(table_body, unroll=64, pitch=pitch),
        grid_spec=pltpu.PrefetchScalarGridSpec(
            num_scalar_prefetch=1,
            grid=(count // nrow,),
            in_specs=[
                pl.BlockSpec(tab.shape, lambda i, s: (0, 0)),
                pl.BlockSpec(part.shape, lambda i, s: (0, 0)),
                pl.BlockSpec(feats.shape, lambda i, s: (0, 0)),
            ],
            out_specs=[
                pl.BlockSpec((nrow, nfeat), lambda i, s: (i, 0)),
                pl.BlockSpec((ncol, nrow), lambda i, s: (0, i)),
            ],
            scratch_shapes=[pltpu.VMEM((nsub * pitch, LANES), jnp.float32)],
        ),
        out_shape=[
            jax.ShapeDtypeStruct((count, nfeat), jnp.bfloat16),
            jax.ShapeDtypeStruct((ncol, count), jnp.float32),
        ],
        compiler_params=pltpu.CompilerParams(vmem_limit_bytes=48 << 20),
        cost_estimate=pl.CostEstimate(
            flops=count * nfeat * 1500, bytes_accessed=count * nfeat * 2, transcendentals=0
        ),
        name="make_table",
    )(starts, tab, part, feats)


def back_body(*refs, nblk):
    mixes, datas, (old_ref, out_ref) = refs[:nblk], refs[nblk : 2 * nblk], refs[2 * nblk :]
    total = old_ref[...]
    for mix_ref, data_ref in zip(mixes, datas):
        total += jnp.dot(mix_ref[...], data_ref[...], preferred_element_type=jnp.float32)
    out_ref[...] = total


def back(mixes, datas, old, half):
    nblk = len(mixes)
    ncol, count = mixes[0].shape
    width = old.shape[1]
    tile = min(512, width)
    steps = width // tile
    at = half * steps
    return pl.pallas_call(
        functools.partial(back_body, nblk=nblk),
        grid=(steps,),
        in_specs=[pl.BlockSpec((ncol, count), lambda f: (0, 0))] * nblk
        + [pl.BlockSpec((count, tile), lambda f: (0, at + f))] * nblk
        + [pl.BlockSpec((ncol, tile), lambda f: (0, f))],
        out_specs=pl.BlockSpec((ncol, tile), lambda f: (0, f)),
        out_shape=jax.ShapeDtypeStruct((ncol, width), jnp.float32),
        compiler_params=pltpu.CompilerParams(vmem_limit_bytes=48 << 20),
        cost_estimate=pl.CostEstimate(
            flops=2 * count * width * ncol * nblk, bytes_accessed=count * width * 2 * nblk, transcendentals=0
        ),
        name="back",
    )(*mixes, *datas, old)


def solve_body(prod_ref, grad_ref, *refs):
    step_ref = refs[-1]
    rank = prod_ref.shape[1]
    inner = prod_ref[:rank, :]
    mat = 0.5 * (inner + inner.T)
    rhs = prod_ref[rank : rank + 1, :]
    eye = (
        lax.broadcasted_iota(jnp.int32, (rank, rank), 0) == lax.broadcasted_iota(jnp.int32, (rank, rank), 1)
    ).astype(jnp.float32)
    col = jnp.sum(eye * rhs, axis=1, keepdims=True)
    row_of = lax.broadcasted_iota(jnp.int32, (rank, 1), 0)
    for k in range(rank):
        lead = mat[k : k + 1, :] / mat[k : k + 1, k : k + 1]
        head = col[k : k + 1, :] / mat[k : k + 1, k : k + 1]
        by = jnp.where(row_of == k, 0.0, mat[:, k : k + 1])
        mat = jnp.where(row_of == k, lead, mat - by * lead)
        col = jnp.where(row_of == k, head, col - by * head)
    at = 0
    for ref in refs[:-1]:
        width = ref.shape[1]
        fit = jnp.sum(ref[...] * col, axis=0, keepdims=True)
        step_ref[:, at : at + width] = (grad_ref[:, at : at + width] - fit) * (1.0 / LAM)
        at += width


def solve(prods, grad, halves):
    return pl.pallas_call(
        solve_body,
        out_shape=jax.ShapeDtypeStruct(grad.shape, jnp.float32),
        compiler_params=pltpu.CompilerParams(vmem_limit_bytes=32 << 20),
        name="solve",
    )(prods, grad, *halves)


def place_body(at_ref, *refs, size):
    for d in range(size):

        @pl.when(pl.program_id(0) == d)
        def _():
            refs[-1][...] = refs[d][...].astype(jnp.float32)


def place(z, parts, half, nhalf, old=None):
    size = len(parts)
    rank, width = parts[0].shape
    extra = [] if old is None else [old]
    return pl.pallas_call(
        functools.partial(place_body, size=size),
        grid_spec=pltpu.PrefetchScalarGridSpec(
            num_scalar_prefetch=1,
            grid=(size,),
            in_specs=[pl.BlockSpec((rank, width), lambda d, at: (0, 0))] * size
            + [pl.BlockSpec(memory_space=pl.ANY)] * len(extra),
            out_specs=pl.BlockSpec((rank, width), lambda d, at: (0, lax.rem(at[0] + d, size) * nhalf + half)),
        ),
        out_shape=jax.ShapeDtypeStruct((rank, width * nhalf * size), jnp.float32),
        input_output_aliases={1 + size: 0} if extra else {},
        compiler_params=pltpu.CompilerParams(vmem_limit_bytes=32 << 20),
        name="place",
    )(z.reshape(1), *parts, *extra)


def shift(x, axis, size, by):
    return lax.ppermute(x, axis, [(i, (i + by) % size) for i in range(size)])


def scatter_sum(x, axis, size):
    if size <= 4:
        total = x[:, 0]
        for d in range(1, size):
            total = total + shift(x[:, d], axis, size, d)
        return total

    def hop(i, acc):
        return shift(acc, axis, size, 1) + lax.dynamic_index_in_dim(x, size - 2 - i, 1, False)

    return lax.fori_loop(0, size - 1, hop, x[:, size - 1])


def collect(x, axis, size, at):
    if size <= 4:
        return jnp.stack([x] + [shift(x, axis, size, -d) for d in range(1, size)], axis=at)

    def hop(cur, _):
        cur = shift(cur, axis, size, -1)
        return cur, cur

    _, rest = lax.scan(hop, x, None, length=size - 1)
    return jnp.moveaxis(jnp.concatenate([x[None], rest], axis=0), 0, at)


def all_sum(x, axis, size):
    if size == 2:
        return x + shift(x, axis, size, 1)
    if size == 4:
        one, two, three = (shift(x, axis, size, -d) for d in (1, 2, 3))
        even = lax.axis_index(axis) % 2 == 0
        return (x + jnp.where(even, one, three)) + (two + jnp.where(even, three, one))
    return lax.psum(x, axis)


def roll_to(x, dim, size, index):
    return lax.dynamic_slice_in_dim(jnp.concatenate([x, x], axis=dim), index, size, dim)


def weigh(margins, labels):
    prob = jax.nn.sigmoid(margins[-1:])
    resid = prob - labels.astype(jnp.float32)
    return jnp.concatenate([prob * (1.0 - prob) * margins[:-1], resid], axis=0).astype(jnp.bfloat16)


def after(x, *deps):
    return lax.optimization_barrier((x, *deps))[0]


def split(x, size, at):
    width = x.shape[1] // size
    return x[:, at * width : (at + 1) * width]


def scatter_rows(x, size):
    if size <= 4:
        return split(x, size, 0), [shift(split(x, size, d), "rows", size, d) for d in range(1, size)]
    return scatter_sum(x.reshape(x.shape[0], size, -1), "rows", size), []


def collect_rows(x, size):
    if size <= 4:
        return [x] + [shift(x, "rows", size, -d) for d in range(1, size)]
    return [collect(x, "rows", size, 1).reshape(x.shape[0], -1)]


def local(sizes, row_seeds, labels, weights, sketch):
    nrows, nsec, nsub = sizes
    count = row_seeds.shape[0]
    rank = sketch.shape[1]
    nfeat = weights.shape[0] // nrows
    z, s, u = lax.axis_index("rows"), lax.axis_index("sec"), lax.axis_index("sub")
    own = z * nfeat
    first = (s * nsub + u) * weights.shape[0] + own

    nchunk = 2
    piece = count // (nchunk * nsec * nsub)
    seeds = row_seeds.reshape(nchunk, nsec, nsub, piece)
    seeds = roll_to(roll_to(seeds, 1, nsec, s), 2, nsub, u)
    starts = window_starts(collect(seeds, "rows", nrows, 3), first)
    labels = labels.reshape(nchunk, nsec, nsub, piece)
    labels = lax.dynamic_slice(labels, (0, s, u, 0), (nchunk, 1, 1, piece)).reshape(nchunk, 1, piece)

    tab = window_table(PRIME + nfeat + LANES)
    cols = first + lax.iota(jnp.int32, nfeat)
    part = (cols * STEP_A % PRIME).astype(jnp.float32).reshape(nfeat // LANES, LANES)
    sketch_t = lax.dynamic_slice_in_dim(sketch.T, own, nfeat, 1)
    own_weights = lax.dynamic_slice_in_dim(weights, own, nfeat, 0)[None]
    feats = jnp.concatenate([sketch_t, own_weights.astype(jnp.bfloat16)], axis=0)
    ncol = rank + 1
    padded = jnp.pad(feats, ((0, -ncol % LANES), (0, 0)))

    order = [(c, du, ds) for c in range(nchunk) for du in reversed(range(nsub)) for ds in reversed(range(nsec))]
    data, marg, from_sub, from_sec, mixed, stage = {}, {}, {}, {}, {}, {}
    older, due = [], []

    def advance(c, at, *deps):
        if at == 0:
            held, come = scatter_rows(sum(from_sec[c][1:], from_sec[c][0]), nrows)
            stage[c] = (held, come)
            return come or [held]
        if at == 1:
            held, come = stage[c]
            held = after(weigh(sum(come, held), labels[c]), *deps)
            stage[c] = collect_rows(held, nrows)
            return stage[c]
        if at == 2:
            mixed[c, 0, 0] = after(jnp.concatenate(stage[c], axis=1), *deps)
            for ds in range(1, nsec):
                mixed[c, 0, ds] = shift(mixed[c, 0, 0], "sec", nsec, -ds)
            return [mixed[c, 0, ds] for ds in range(1, nsec)]
        if at == 3:
            half = jnp.concatenate([mixed[c, 0, ds] for ds in range(nsec)], axis=1)
            half = after(half, *deps)
            for du in range(1, nsub):
                come = shift(half, "sub", nsub, -du)
                for ds in range(nsec):
                    mixed[c, du, ds] = split(come, nsec, ds)
            return [mixed[c, nsub - 1, 0]]
        return []

    running = []

    def boundary(*deps):
        out = []
        for chunk in list(running):
            out += advance(chunk[0], chunk[1], *deps)
            chunk[1] += 1
            if chunk[1] > 3:
                running.remove(chunk)
        return out

    last = []
    for c, du, ds in order:
        begin = after(starts[c, ds, du].reshape(-1), *last, *older)
        data[c, du, ds], marg[c, du, ds] = make_table(begin, tab, part, padded, ncol)
        last = [marg[c, du, ds]]
        older, due = due, boundary()
        if du:
            from_sub[c, du, ds] = shift(marg[c, du, ds], "sub", nsub, du)
            due.append(from_sub[c, du, ds])
        else:
            summed = sum([from_sub[c, e, ds] for e in range(1, nsub)], marg[c, du, ds])
            if ds:
                from_sec.setdefault(c, []).append(shift(summed, "sec", nsec, ds))
                due.append(from_sec[c][-1])
            else:
                from_sec[c].insert(0, summed)
                running.append([c, 0])
                if (c, du, ds) == order[-1]:
                    due += boundary()

    nhalf = 2
    width = nfeat // nhalf
    totals = [jnp.zeros((ncol, width), jnp.float32)] * nhalf
    sketch_f = sketch_t.astype(jnp.float32)
    grads, parts, blocks, wide, lefts = [None] * nhalf, [None] * nhalf, [None] * nhalf, [None] * nhalf, [None] * nhalf

    def product(c, dus, half):
        names = [(c, du, ds) for du in dus for ds in range(nsec)]
        while any(name not in mixed for name in names):
            due.extend(boundary())
        mixes = [mixed[name] for name in names]
        mixes[0] = after(mixes[0], *older)
        totals[half] = back(mixes, [data[name] for name in names], totals[half], half)

    def close(half, *deps):
        total = totals[half] * SCALE
        cut = slice(half * width, (half + 1) * width)
        grads[half] = total[rank:] + LAM * own_weights[:, cut]
        parts[half] = total[:rank] + LAM * sketch_f[:, cut]
        lefts[half] = jnp.concatenate([LAM * sketch_f[:, cut] + parts[half], grads[half]], axis=0)
        blocks[half] = parts[half].astype(jnp.bfloat16)

    def send(half, ds, *deps):
        block = after(blocks[half], *deps)
        wide[half] = wide[half] or {0: blocks[half]}
        for d in ds:
            wide[half][d] = shift(block, "rows", nrows, -d)

    plan = [(0, [du], half) for half in range(nhalf) for du in range(nsub)]
    for c, dus, half in plan[:-1]:
        product(c, dus, half)
        older, due = due, boundary(totals[half])
    product(nchunk - 1, range(nsub), 0)
    close(0)
    direct = nrows <= 4
    if direct:
        send(0, range(1, nrows))
    c, dus, half = plan[-1]
    older = [totals[0]]
    product(c, dus, half)
    older = [wide[0][1]] if direct else []
    product(nchunk - 1, range(nsub), 1)
    close(1)
    if direct:
        send(1, [1])

    prods = sum(
        lax.dot_general(left, part, (((1,), (1,)), ((), ())), precision=lax.Precision.HIGHEST)
        for left, part in zip(lefts, parts)
    )
    prods = all_sum(prods, "sub", nsub)
    if direct:
        prods = after(prods, wide[0][nrows - 1])
    prods = all_sum(prods, "sec", nsec)
    if direct:
        prods = after(prods, *wide[0].values(), wide[1][1])
    prods = all_sum(prods, "rows", nrows)
    if direct:
        send(1, range(2, nrows), prods)
    step = solve(prods, jnp.concatenate(grads, axis=1), parts)

    def spread(x):
        parts = roll_to(collect(x, "rows", nrows, 0), 0, nrows, (nrows - z) % nrows)
        return jnp.moveaxis(parts, 0, 1).reshape(x.shape[0], -1).astype(jnp.float32)

    if direct:
        step = after(step, wide[1][nrows - 1])
    step = spread(step)[0]
    if direct:
        wide[1][0] = after(wide[1][0], step)
        out = None
        for half in range(nhalf):
            out = place(z, [wide[half][d] for d in range(nrows)], half, nhalf, out)
    else:
        out = spread(jnp.concatenate(blocks, axis=1))
    return (step, out.T)


def solution(mesh):
    placed = (
        P(("group", "rows")),
        P(("group", "rows")),
        P(("group", "sec", "sub")),
        P(("sec", "sub"), None),
    )
    sizes = tuple(mesh.shape[name] for name in ("rows", "sec", "sub"))
    return jax.shard_map(
        functools.partial(local, sizes),
        mesh=mesh,
        in_specs=placed,
        out_specs=(P(("group", "sec", "sub")), P(("group", "sec", "sub"), None)),
        check_vma=False,
    )
```

```python
import functools

import jax
import jax.numpy as jnp
from jax import lax
from jax.experimental import pallas as pl
from jax.experimental.pallas import tpu as pltpu
from jax.sharding import PartitionSpec as P

PRIME = 65521
FOLD = 46337
STEP_A = 30011
STEP_B = 16411
SHIFT = STEP_B * pow(STEP_A, -1, PRIME) % PRIME
LAM = 0.05
SCALE = 1.0 / 1024.0
LANES = 128
LEVEL = jnp.float8_e4m3fn


def window_table(length):
    rows = -(-length // (8 * LANES)) * 8
    n = lax.broadcasted_iota(jnp.int32, (rows, LANES), 0) * LANES + lax.broadcasted_iota(
        jnp.int32, (rows, LANES), 1
    )
    mixer = n % PRIME * STEP_A % PRIME
    folded = mixer % FOLD
    entry = (folded * folded % PRIME * 31 + 7) % PRIME
    return entry.astype(jnp.float32) - (PRIME - 0.5)


def window_starts(seeds, first):
    high = seeds * (SHIFT // 256) % PRIME
    return (high * 256 + seeds * (SHIFT % 256) + first) % PRIME


def whole_vmem():
    return pl.BlockSpec(memory_space=pltpu.VMEM)


def table_body(start_ref, tab_ref, a_ref, feat_ref, data_ref, marg_ref, scr, wide, *, unroll, pitch):
    nrow, nfeat = wide.shape
    nsub = nfeat // LANES
    high = min(8, nsub)
    lane = lax.broadcasted_iota(jnp.int32, (high, LANES), 1)
    base = pl.program_id(0) * nrow
    part = a_ref[...]

    def samples(group, carry):
        for u in range(unroll):
            row = group * unroll + u
            start = start_ref[base + row]
            top = start >> 7
            off = start & (LANES - 1)
            early = lane < off
            one = tab_ref[pl.ds(top, nsub), :]
            two = tab_ref[pl.ds(top + 1, nsub), :]
            for v in range(0, nsub, high):
                win = jnp.where(early, two[v : v + high], one[v : v + high])
                win = pltpu.roll(win, LANES - off, 1)
                level = (win + part[v : v + high]).astype(jnp.int32) & 15
                scr[pl.ds(row + v * pitch, high, stride=pitch), :] = level.astype(jnp.float32) - 7.5
        return carry

    lax.fori_loop(0, nrow // unroll, samples, 0)
    for r in range(nsub):
        cut = slice(r * LANES, (r + 1) * LANES)
        level = scr[pl.ds(r * pitch, nrow), :]
        wide[:, cut] = level.astype(jnp.bfloat16)
        data_ref[pl.ds(pl.multiple_of(base, nrow), nrow), cut] = level.astype(LEVEL)
    marg = lax.dot_general(
        wide[...], feat_ref[...], (((1,), (1,)), ((), ())), preferred_element_type=jnp.float32
    )
    marg_ref[...] = SCALE * marg.T[: marg_ref.shape[0]]


def make_table(starts, tab, part, feats, ncol):
    count = starts.shape[0]
    nsub = part.shape[0]
    nfeat = nsub * LANES
    nrow = min(256, count)
    pitch = nrow + 8
    return pl.pallas_call(
        functools.partial(table_body, unroll=64, pitch=pitch),
        grid_spec=pltpu.PrefetchScalarGridSpec(
            num_scalar_prefetch=1,
            grid=(count // nrow,),
            in_specs=[
                pl.BlockSpec(tab.shape, lambda i, s: (0, 0)),
                pl.BlockSpec(part.shape, lambda i, s: (0, 0)),
                pl.BlockSpec(feats.shape, lambda i, s: (0, 0)),
            ],
            out_specs=[
                whole_vmem(),
                pl.BlockSpec((ncol, nrow), lambda i, s: (0, i)),
            ],
            scratch_shapes=[
                pltpu.VMEM((nsub * pitch, LANES), jnp.float32),
                pltpu.VMEM((nrow, nfeat), jnp.bfloat16),
            ],
        ),
        out_shape=[
            pltpu.VMEM((count, nfeat), LEVEL),
            jax.ShapeDtypeStruct((ncol, count), jnp.float32),
        ],
        compiler_params=pltpu.CompilerParams(vmem_limit_bytes=12 << 20),
        cost_estimate=pl.CostEstimate(
            flops=count * nfeat * 1500, bytes_accessed=count * nfeat * 2, transcendentals=0
        ),
        name="make_table",
    )(starts, tab, part, feats)


def back_body(*refs, nblk, tile, half):
    mixes, datas, (old_ref, out_ref) = refs[:nblk], refs[nblk : 2 * nblk], refs[2 * nblk :]
    width = out_ref.shape[1]
    for at in range(0, width, tile):
        total = old_ref[:, at : at + tile]
        for mix_ref, data_ref in zip(mixes, datas):
            level = data_ref[:, half * width + at : half * width + at + tile].astype(jnp.bfloat16)
            total += jnp.dot(mix_ref[...], level, preferred_element_type=jnp.float32)
        out_ref[:, at : at + tile] = total


def back(mixes, datas, old, half):
    nblk = len(mixes)
    ncol, count = mixes[0].shape
    width = old.shape[1]
    return pl.pallas_call(
        functools.partial(back_body, nblk=nblk, tile=min(512, width), half=half),
        in_specs=[whole_vmem()] * (2 * nblk + 1),
        out_specs=whole_vmem(),
        out_shape=jax.ShapeDtypeStruct((ncol, width), jnp.float32),
        compiler_params=pltpu.CompilerParams(vmem_limit_bytes=12 << 20),
        cost_estimate=pl.CostEstimate(
            flops=2 * count * width * ncol * nblk, bytes_accessed=count * width * nblk, transcendentals=0
        ),
        name="back",
    )(*mixes, *datas, old)


def solve_body(prod_ref, grad_ref, *refs):
    step_ref = refs[-1]
    rank = prod_ref.shape[1]
    inner = prod_ref[:rank, :]
    mat = 0.5 * (inner + inner.T)
    rhs = prod_ref[rank : rank + 1, :]
    eye = (
        lax.broadcasted_iota(jnp.int32, (rank, rank), 0) == lax.broadcasted_iota(jnp.int32, (rank, rank), 1)
    ).astype(jnp.float32)
    col = jnp.sum(eye * rhs, axis=1, keepdims=True)
    row_of = lax.broadcasted_iota(jnp.int32, (rank, 1), 0)
    for k in range(rank):
        lead = mat[k : k + 1, :] / mat[k : k + 1, k : k + 1]
        head = col[k : k + 1, :] / mat[k : k + 1, k : k + 1]
        by = jnp.where(row_of == k, 0.0, mat[:, k : k + 1])
        mat = jnp.where(row_of == k, lead, mat - by * lead)
        col = jnp.where(row_of == k, head, col - by * head)
    at = 0
    for ref in refs[:-1]:
        width = ref.shape[1]
        fit = jnp.sum(ref[...] * col, axis=0, keepdims=True)
        step_ref[:, at : at + width] = (grad_ref[:, at : at + width] - fit) * (1.0 / LAM)
        at += width


def solve(prods, grad, halves):
    return pl.pallas_call(
        solve_body,
        out_shape=jax.ShapeDtypeStruct(grad.shape, jnp.float32),
        compiler_params=pltpu.CompilerParams(vmem_limit_bytes=8 << 20),
        name="solve",
    )(prods, grad, *halves)


def place_body(at_ref, *refs, size):
    for d in range(size):

        @pl.when(pl.program_id(0) == d)
        def _():
            refs[-1][...] = refs[d][...].astype(jnp.float32)


def place(z, parts, half, nhalf, old=None):
    size = len(parts)
    rank, width = parts[0].shape
    extra = [] if old is None else [old]
    return pl.pallas_call(
        functools.partial(place_body, size=size),
        grid_spec=pltpu.PrefetchScalarGridSpec(
            num_scalar_prefetch=1,
            grid=(size,),
            in_specs=[pl.BlockSpec((rank, width), lambda d, at: (0, 0))] * size
            + [pl.BlockSpec(memory_space=pl.ANY)] * len(extra),
            out_specs=pl.BlockSpec((rank, width), lambda d, at: (0, lax.rem(at[0] + d, size) * nhalf + half)),
        ),
        out_shape=jax.ShapeDtypeStruct((rank, width * nhalf * size), jnp.float32),
        input_output_aliases={1 + size: 0} if extra else {},
        compiler_params=pltpu.CompilerParams(vmem_limit_bytes=8 << 20),
        name="place",
    )(z.reshape(1), *parts, *extra)


def shift(x, axis, size, by):
    return lax.ppermute(x, axis, [(i, (i + by) % size) for i in range(size)])


def scatter_sum(x, axis, size):
    if size <= 4:
        total = x[:, 0]
        for d in range(1, size):
            total = total + shift(x[:, d], axis, size, d)
        return total

    def hop(i, acc):
        return shift(acc, axis, size, 1) + lax.dynamic_index_in_dim(x, size - 2 - i, 1, False)

    return lax.fori_loop(0, size - 1, hop, x[:, size - 1])


def collect(x, axis, size, at):
    if size <= 4:
        return jnp.stack([x] + [shift(x, axis, size, -d) for d in range(1, size)], axis=at)

    def hop(cur, _):
        cur = shift(cur, axis, size, -1)
        return cur, cur

    _, rest = lax.scan(hop, x, None, length=size - 1)
    return jnp.moveaxis(jnp.concatenate([x[None], rest], axis=0), 0, at)


def all_sum(x, axis, size):
    if size == 2:
        return x + shift(x, axis, size, 1)
    if size == 4:
        one, two, three = (shift(x, axis, size, -d) for d in (1, 2, 3))
        even = lax.axis_index(axis) % 2 == 0
        return (x + jnp.where(even, one, three)) + (two + jnp.where(even, three, one))
    return lax.psum(x, axis)


def roll_to(x, dim, size, index):
    return lax.dynamic_slice_in_dim(jnp.concatenate([x, x], axis=dim), index, size, dim)


def weigh(margins, labels):
    prob = jax.nn.sigmoid(margins[-1:])
    resid = prob - labels.astype(jnp.float32)
    return jnp.concatenate([prob * (1.0 - prob) * margins[:-1], resid], axis=0).astype(jnp.bfloat16)


def after(x, *deps):
    return lax.optimization_barrier((x, *deps))[0]


def split(x, size, at):
    width = x.shape[1] // size
    return x[:, at * width : (at + 1) * width]


def scatter_rows(x, size):
    if size <= 4:
        return split(x, size, 0), [shift(split(x, size, d), "rows", size, d) for d in range(1, size)]
    return scatter_sum(x.reshape(x.shape[0], size, -1), "rows", size), []


def collect_rows(x, size):
    if size <= 4:
        return [x] + [shift(x, "rows", size, -d) for d in range(1, size)]
    return [collect(x, "rows", size, 1).reshape(x.shape[0], -1)]


def local(sizes, row_seeds, labels, weights, sketch):
    nrows, nsec, nsub = sizes
    count = row_seeds.shape[0]
    rank = sketch.shape[1]
    nfeat = weights.shape[0] // nrows
    z, s, u = lax.axis_index("rows"), lax.axis_index("sec"), lax.axis_index("sub")
    own = z * nfeat
    first = (s * nsub + u) * weights.shape[0] + own

    nchunk = 2
    piece = count // (nchunk * nsec * nsub)
    seeds = row_seeds.reshape(nchunk, nsec, nsub, piece)
    seeds = roll_to(roll_to(seeds, 1, nsec, s), 2, nsub, u)
    starts = window_starts(collect(seeds, "rows", nrows, 3), first)
    labels = labels.reshape(nchunk, nsec, nsub, piece)
    labels = lax.dynamic_slice(labels, (0, s, u, 0), (nchunk, 1, 1, piece)).reshape(nchunk, 1, piece)

    tab = window_table(PRIME + nfeat + LANES)
    cols = first + lax.iota(jnp.int32, nfeat)
    part = (cols * STEP_A % PRIME).astype(jnp.float32).reshape(nfeat // LANES, LANES)
    sketch_t = lax.dynamic_slice_in_dim(sketch.T, own, nfeat, 1)
    own_weights = lax.dynamic_slice_in_dim(weights, own, nfeat, 0)[None]
    feats = jnp.concatenate([sketch_t, own_weights.astype(jnp.bfloat16)], axis=0)
    ncol = rank + 1
    padded = jnp.pad(feats, ((0, -ncol % LANES), (0, 0)))

    order = [(c, du, ds) for c in range(nchunk) for du in reversed(range(nsub)) for ds in reversed(range(nsec))]
    data, marg, from_sub, from_sec, mixed, stage = {}, {}, {}, {}, {}, {}
    older, due = [], []

    def advance(c, at, *deps):
        if at == 0:
            held, come = scatter_rows(sum(from_sec[c][1:], from_sec[c][0]), nrows)
            stage[c] = (held, come)
            return come or [held]
        if at == 1:
            held, come = stage[c]
            held = after(held, *deps)
            come = [after(x, *deps) for x in come]
            stage[c] = collect_rows(weigh(sum(come, held), labels[c]), nrows)
            return stage[c]
        if at == 2:
            mixed[c, 0, 0] = jnp.concatenate([after(x, *deps) for x in stage[c]], axis=1)
            for ds in range(1, nsec):
                mixed[c, 0, ds] = shift(mixed[c, 0, 0], "sec", nsec, -ds)
            return [mixed[c, 0, ds] for ds in range(1, nsec)]
        if at == 3:
            half = jnp.concatenate([after(mixed[c, 0, ds], *deps) for ds in range(nsec)], axis=1)
            for du in range(1, nsub):
                come = shift(half, "sub", nsub, -du)
                for ds in range(nsec):
                    mixed[c, du, ds] = split(come, nsec, ds)
            return [mixed[c, nsub - 1, 0]]
        return []

    running = []

    def boundary(*deps):
        out = []
        for chunk in list(running):
            out += advance(chunk[0], chunk[1], *deps)
            chunk[1] += 1
            if chunk[1] > 3:
                running.remove(chunk)
        return out

    last = []
    for c, du, ds in order:
        begin = after(starts[c, ds, du].reshape(-1), *last, *older)
        data[c, du, ds], marg[c, du, ds] = make_table(begin, tab, part, padded, ncol)
        last = [marg[c, du, ds]]
        older, due = due, boundary(*last)
        if du:
            from_sub[c, du, ds] = shift(marg[c, du, ds], "sub", nsub, du)
            due.append(from_sub[c, du, ds])
        else:
            summed = sum([from_sub[c, e, ds] for e in range(1, nsub)], marg[c, du, ds])
            if ds:
                from_sec.setdefault(c, []).append(shift(summed, "sec", nsec, ds))
                due.append(from_sec[c][-1])
            else:
                from_sec[c].insert(0, summed)
                running.append([c, 0])
                if (c, du, ds) == order[-1]:
                    due += boundary()

    nhalf = 2
    width = nfeat // nhalf
    totals = [jnp.zeros((ncol, width), jnp.float32)] * nhalf
    sketch_f = sketch_t.astype(jnp.float32)
    grads, parts, blocks, wide, lefts = [None] * nhalf, [None] * nhalf, [None] * nhalf, [None] * nhalf, [None] * nhalf

    def product(c, dus, half):
        names = [(c, du, ds) for du in dus for ds in range(nsec)]
        while any(name not in mixed for name in names):
            due.extend(boundary())
        mixes = [mixed[name] for name in names]
        mixes[0] = after(mixes[0], *older)
        totals[half] = back(mixes, [data[name] for name in names], totals[half], half)

    def close(half, *deps):
        total = totals[half] * SCALE
        cut = slice(half * width, (half + 1) * width)
        grads[half] = total[rank:] + LAM * own_weights[:, cut]
        parts[half] = total[:rank] + LAM * sketch_f[:, cut]
        lefts[half] = jnp.concatenate([LAM * sketch_f[:, cut] + parts[half], grads[half]], axis=0)
        blocks[half] = parts[half].astype(jnp.bfloat16)

    def send(half, ds, *deps):
        block = after(blocks[half], *deps)
        wide[half] = wide[half] or {0: blocks[half]}
        for d in ds:
            wide[half][d] = shift(block, "rows", nrows, -d)

    plan = [(0, [du], half) for half in range(nhalf) for du in range(nsub)]
    for c, dus, half in plan[:-1]:
        product(c, dus, half)
        older, due = due, boundary(totals[half])
    product(nchunk - 1, range(nsub), 0)
    close(0)
    direct = nrows <= 4
    if direct:
        send(0, range(1, nrows))
    c, dus, half = plan[-1]
    older = [totals[0]]
    product(c, dus, half)
    older = []
    for du in range(nsub):
        product(nchunk - 1, [du], 1)
        older = [wide[0][1]] if direct else []
    close(1)
    if direct:
        send(1, [1])

    prods = sum(
        lax.dot_general(left, part, (((1,), (1,)), ((), ())), precision=lax.Precision.HIGHEST)
        for left, part in zip(lefts, parts)
    )
    if direct:
        prods = after(prods, wide[0][1])
    prods = all_sum(prods, "sub", nsub)
    if direct:
        prods = after(prods, wide[0][nrows - 1])
    prods = all_sum(prods, "sec", nsec)
    if direct:
        prods = after(prods, *wide[0].values(), wide[1][1])
    prods = all_sum(prods, "rows", nrows)
    if direct:
        send(1, range(2, nrows), prods)
    step = solve(prods, jnp.concatenate(grads, axis=1), parts)

    def spread(x):
        parts = roll_to(collect(x, "rows", nrows, 0), 0, nrows, (nrows - z) % nrows)
        return jnp.moveaxis(parts, 0, 1).reshape(x.shape[0], -1).astype(jnp.float32)

    if direct:
        step = after(step, wide[1][nrows - 1])
    step = spread(step)[0]
    if direct:
        wide[1][0] = after(wide[1][0], step)
        out = None
        for half in range(nhalf):
            out = place(z, [wide[half][d] for d in range(nrows)], half, nhalf, out)
    else:
        out = spread(jnp.concatenate(blocks, axis=1))
    return (step, out.T)


def solution(mesh):
    placed = (
        P(("group", "rows")),
        P(("group", "rows")),
        P(("group", "sec", "sub")),
        P(("sec", "sub"), None),
    )
    sizes = tuple(mesh.shape[name] for name in ("rows", "sec", "sub"))
    return jax.shard_map(
        functools.partial(local, sizes),
        mesh=mesh,
        in_specs=placed,
        out_specs=(P(("group", "sec", "sub")), P(("group", "sec", "sub"), None)),
        check_vma=False,
    )
```

```python
import functools

import jax
import jax.numpy as jnp
from jax import lax
from jax.experimental import pallas as pl
from jax.experimental.pallas import tpu as pltpu
from jax.sharding import PartitionSpec as P

PRIME = 65521
FOLD = 46337
STEP_A = 30011
STEP_B = 16411
SHIFT = STEP_B * pow(STEP_A, -1, PRIME) % PRIME
LAM = 0.05
SCALE = 1.0 / 1024.0
LANES = 128
LEVEL = jnp.float8_e4m3fn


def window_table(length):
    rows = -(-length // (8 * LANES)) * 8
    n = lax.broadcasted_iota(jnp.int32, (rows, LANES), 0) * LANES + lax.broadcasted_iota(
        jnp.int32, (rows, LANES), 1
    )
    mixer = n % PRIME * STEP_A % PRIME
    folded = mixer % FOLD
    entry = (folded * folded % PRIME * 31 + 7) % PRIME
    return entry.astype(jnp.float32) - (PRIME - 0.5)


def window_starts(seeds, first):
    high = seeds * (SHIFT // 256) % PRIME
    return (high * 256 + seeds * (SHIFT % 256) + first) % PRIME


def whole_vmem():
    return pl.BlockSpec(memory_space=pltpu.VMEM)


def table_body(start_ref, tab_ref, a_ref, feat_ref, data_ref, marg_ref, scr, wide, *, unroll, pitch):
    nrow, nfeat = wide.shape
    nsub = nfeat // LANES
    high = min(8, nsub)
    lane = lax.broadcasted_iota(jnp.int32, (high, LANES), 1)
    base = pl.program_id(0) * nrow
    part = a_ref[...]

    def samples(group, carry):
        for u in range(unroll):
            row = group * unroll + u
            start = start_ref[base + row]
            top = start >> 7
            off = start & (LANES - 1)
            early = lane < off
            one = tab_ref[pl.ds(top, nsub), :]
            two = tab_ref[pl.ds(top + 1, nsub), :]
            for v in range(0, nsub, high):
                win = jnp.where(early, two[v : v + high], one[v : v + high])
                win = pltpu.roll(win, LANES - off, 1)
                level = (win + part[v : v + high]).astype(jnp.int32) & 15
                scr[pl.ds(row + v * pitch, high, stride=pitch), :] = level.astype(jnp.float32) - 7.5
        return carry

    lax.fori_loop(0, nrow // unroll, samples, 0)
    for r in range(nsub):
        cut = slice(r * LANES, (r + 1) * LANES)
        level = scr[pl.ds(r * pitch, nrow), :]
        wide[:, cut] = level.astype(jnp.bfloat16)
        data_ref[pl.ds(pl.multiple_of(base, nrow), nrow), cut] = level.astype(LEVEL)
    marg = lax.dot_general(
        wide[...], feat_ref[...], (((1,), (1,)), ((), ())), preferred_element_type=jnp.float32
    )
    marg_ref[...] = SCALE * marg.T[: marg_ref.shape[0]]


def make_table(starts, tab, part, feats, ncol):
    count = starts.shape[0]
    nsub = part.shape[0]
    nfeat = nsub * LANES
    nrow = min(256, count)
    pitch = nrow + 8
    return pl.pallas_call(
        functools.partial(table_body, unroll=min(128, nrow), pitch=pitch),
        grid_spec=pltpu.PrefetchScalarGridSpec(
            num_scalar_prefetch=1,
            grid=(count // nrow,),
            in_specs=[
                pl.BlockSpec(tab.shape, lambda i, s: (0, 0)),
                pl.BlockSpec(part.shape, lambda i, s: (0, 0)),
                pl.BlockSpec(feats.shape, lambda i, s: (0, 0)),
            ],
            out_specs=[
                whole_vmem(),
                pl.BlockSpec((ncol, nrow), lambda i, s: (0, i)),
            ],
            scratch_shapes=[
                pltpu.VMEM((nsub * pitch, LANES), jnp.float32),
                pltpu.VMEM((nrow, nfeat), jnp.bfloat16),
            ],
        ),
        out_shape=[
            pltpu.VMEM((count, nfeat), LEVEL),
            jax.ShapeDtypeStruct((ncol, count), jnp.float32),
        ],
        compiler_params=pltpu.CompilerParams(vmem_limit_bytes=12 << 20),
        cost_estimate=pl.CostEstimate(
            flops=count * nfeat * 1500, bytes_accessed=count * nfeat * 2, transcendentals=0
        ),
        name="make_table",
    )(starts, tab, part, feats)


def back_body(*refs, nblk, tile, half):
    mixes, datas, (old_ref, out_ref) = refs[:nblk], refs[nblk : 2 * nblk], refs[2 * nblk :]
    width = out_ref.shape[1]
    for at in range(0, width, tile):
        total = old_ref[:, at : at + tile]
        for mix_ref, data_ref in zip(mixes, datas):
            level = data_ref[:, half * width + at : half * width + at + tile].astype(jnp.bfloat16)
            total += jnp.dot(mix_ref[...], level, preferred_element_type=jnp.float32)
        out_ref[:, at : at + tile] = total


def back(mixes, datas, old, half):
    nblk = len(mixes)
    ncol, count = mixes[0].shape
    width = old.shape[1]
    return pl.pallas_call(
        functools.partial(back_body, nblk=nblk, tile=min(512, width), half=half),
        in_specs=[whole_vmem()] * (2 * nblk + 1),
        out_specs=whole_vmem(),
        out_shape=jax.ShapeDtypeStruct((ncol, width), jnp.float32),
        compiler_params=pltpu.CompilerParams(vmem_limit_bytes=12 << 20),
        cost_estimate=pl.CostEstimate(
            flops=2 * count * width * ncol * nblk, bytes_accessed=count * width * nblk, transcendentals=0
        ),
        name="back",
    )(*mixes, *datas, old)


def solve_body(prod_ref, grad_ref, *refs):
    step_ref = refs[-1]
    rank = prod_ref.shape[1]
    inner = prod_ref[:rank, :]
    mat = 0.5 * (inner + inner.T)
    rhs = prod_ref[rank : rank + 1, :]
    eye = (
        lax.broadcasted_iota(jnp.int32, (rank, rank), 0) == lax.broadcasted_iota(jnp.int32, (rank, rank), 1)
    ).astype(jnp.float32)
    col = jnp.sum(eye * rhs, axis=1, keepdims=True)
    row_of = lax.broadcasted_iota(jnp.int32, (rank, 1), 0)
    for k in range(rank):
        lead = mat[k : k + 1, :] / mat[k : k + 1, k : k + 1]
        head = col[k : k + 1, :] / mat[k : k + 1, k : k + 1]
        by = jnp.where(row_of == k, 0.0, mat[:, k : k + 1])
        mat = jnp.where(row_of == k, lead, mat - by * lead)
        col = jnp.where(row_of == k, head, col - by * head)
    at = 0
    for ref in refs[:-1]:
        width = ref.shape[1]
        fit = jnp.sum(ref[...] * col, axis=0, keepdims=True)
        step_ref[:, at : at + width] = (grad_ref[:, at : at + width] - fit) * (1.0 / LAM)
        at += width


def solve(prods, grad, halves):
    return pl.pallas_call(
        solve_body,
        out_shape=jax.ShapeDtypeStruct(grad.shape, jnp.float32),
        compiler_params=pltpu.CompilerParams(vmem_limit_bytes=8 << 20),
        name="solve",
    )(prods, grad, *halves)


def place_body(at_ref, *refs, size):
    for d in range(size):

        @pl.when(pl.program_id(0) == d)
        def _():
            refs[-1][...] = refs[d][...].astype(jnp.float32)


def place(z, parts, half, nhalf, old=None):
    size = len(parts)
    rank, width = parts[0].shape
    extra = [] if old is None else [old]
    return pl.pallas_call(
        functools.partial(place_body, size=size),
        grid_spec=pltpu.PrefetchScalarGridSpec(
            num_scalar_prefetch=1,
            grid=(size,),
            in_specs=[pl.BlockSpec((rank, width), lambda d, at: (0, 0))] * size
            + [pl.BlockSpec(memory_space=pl.ANY)] * len(extra),
            out_specs=pl.BlockSpec((rank, width), lambda d, at: (0, lax.rem(at[0] + d, size) * nhalf + half)),
        ),
        out_shape=jax.ShapeDtypeStruct((rank, width * nhalf * size), jnp.float32),
        input_output_aliases={1 + size: 0} if extra else {},
        compiler_params=pltpu.CompilerParams(vmem_limit_bytes=8 << 20),
        name="place",
    )(z.reshape(1), *parts, *extra)


def shift(x, axis, size, by):
    return lax.ppermute(x, axis, [(i, (i + by) % size) for i in range(size)])


def scatter_sum(x, axis, size):
    if size <= 4:
        total = x[:, 0]
        for d in range(1, size):
            total = total + shift(x[:, d], axis, size, d)
        return total

    def hop(i, acc):
        return shift(acc, axis, size, 1) + lax.dynamic_index_in_dim(x, size - 2 - i, 1, False)

    return lax.fori_loop(0, size - 1, hop, x[:, size - 1])


def collect(x, axis, size, at):
    if size <= 4:
        return jnp.stack([x] + [shift(x, axis, size, -d) for d in range(1, size)], axis=at)

    def hop(cur, _):
        cur = shift(cur, axis, size, -1)
        return cur, cur

    _, rest = lax.scan(hop, x, None, length=size - 1)
    return jnp.moveaxis(jnp.concatenate([x[None], rest], axis=0), 0, at)


def all_sum(x, axis, size):
    if size == 2:
        return x + shift(x, axis, size, 1)
    if size == 4:
        one, two, three = (shift(x, axis, size, -d) for d in (1, 2, 3))
        even = lax.axis_index(axis) % 2 == 0
        return (x + jnp.where(even, one, three)) + (two + jnp.where(even, three, one))
    return lax.psum(x, axis)


def roll_to(x, dim, size, index):
    return lax.dynamic_slice_in_dim(jnp.concatenate([x, x], axis=dim), index, size, dim)


def weigh(margins, labels):
    prob = jax.nn.sigmoid(margins[-1:])
    resid = prob - labels.astype(jnp.float32)
    return jnp.concatenate([prob * (1.0 - prob) * margins[:-1], resid], axis=0).astype(jnp.bfloat16)


def after(x, *deps):
    return lax.optimization_barrier((x, *deps))[0]


def split(x, size, at):
    width = x.shape[1] // size
    return x[:, at * width : (at + 1) * width]


def scatter_rows(x, size):
    if size <= 4:
        return split(x, size, 0), [shift(split(x, size, d), "rows", size, d) for d in range(1, size)]
    return scatter_sum(x.reshape(x.shape[0], size, -1), "rows", size), []


def collect_rows(x, size):
    if size <= 4:
        return [x] + [shift(x, "rows", size, -d) for d in range(1, size)]
    return [collect(x, "rows", size, 1).reshape(x.shape[0], -1)]


def local(sizes, row_seeds, labels, weights, sketch):
    nrows, nsec, nsub = sizes
    count = row_seeds.shape[0]
    rank = sketch.shape[1]
    nfeat = weights.shape[0] // nrows
    z, s, u = lax.axis_index("rows"), lax.axis_index("sec"), lax.axis_index("sub")
    own = z * nfeat
    first = (s * nsub + u) * weights.shape[0] + own

    nchunk = 2
    piece = count // (nchunk * nsec * nsub)
    seeds = row_seeds.reshape(nchunk, nsec, nsub, piece)
    seeds = roll_to(roll_to(seeds, 1, nsec, s), 2, nsub, u)
    starts = window_starts(collect(seeds, "rows", nrows, 3), first)
    labels = labels.reshape(nchunk, nsec, nsub, piece)
    labels = lax.dynamic_slice(labels, (0, s, u, 0), (nchunk, 1, 1, piece)).reshape(nchunk, 1, piece)

    tab = window_table(PRIME + nfeat + LANES)
    cols = first + lax.iota(jnp.int32, nfeat)
    part = (cols * STEP_A % PRIME).astype(jnp.float32).reshape(nfeat // LANES, LANES)
    sketch_t = lax.dynamic_slice_in_dim(sketch.T, own, nfeat, 1)
    own_weights = lax.dynamic_slice_in_dim(weights, own, nfeat, 0)[None]
    feats = jnp.concatenate([sketch_t, own_weights.astype(jnp.bfloat16)], axis=0)
    ncol = rank + 1
    padded = jnp.pad(feats, ((0, -ncol % LANES), (0, 0)))

    order = [(c, du, ds) for c in range(nchunk) for du in reversed(range(nsub)) for ds in reversed(range(nsec))]
    data, marg, from_sub, from_sec, mixed, stage = {}, {}, {}, {}, {}, {}
    older, due = [], []

    def advance(c, at, *deps):
        if at == 0:
            held, come = scatter_rows(sum(from_sec[c][1:], from_sec[c][0]), nrows)
            stage[c] = (held, come)
            return come or [held]
        if at == 1:
            held, come = stage[c]
            held = after(held, *deps)
            come = [after(x, *deps) for x in come]
            stage[c] = collect_rows(weigh(sum(come, held), labels[c]), nrows)
            return stage[c]
        if at == 2:
            mixed[c, 0, 0] = jnp.concatenate([after(x, *deps) for x in stage[c]], axis=1)
            for ds in range(1, nsec):
                mixed[c, 0, ds] = shift(mixed[c, 0, 0], "sec", nsec, -ds)
            return [mixed[c, 0, ds] for ds in range(1, nsec)]
        if at == 3:
            half = jnp.concatenate([after(mixed[c, 0, ds], *deps) for ds in range(nsec)], axis=1)
            for du in range(1, nsub):
                come = shift(half, "sub", nsub, -du)
                for ds in range(nsec):
                    mixed[c, du, ds] = split(come, nsec, ds)
            return [mixed[c, nsub - 1, 0]]
        return []

    running = []

    def boundary(*deps):
        out = []
        for chunk in list(running):
            out += advance(chunk[0], chunk[1], *deps)
            chunk[1] += 1
            if chunk[1] > 3:
                running.remove(chunk)
        return out

    last = []
    for c, du, ds in order:
        begin = after(starts[c, ds, du].reshape(-1), *last, *older)
        data[c, du, ds], marg[c, du, ds] = make_table(begin, tab, part, padded, ncol)
        last = [marg[c, du, ds]]
        older, due = due, boundary(*last)
        if du:
            from_sub[c, du, ds] = shift(marg[c, du, ds], "sub", nsub, du)
            due.append(from_sub[c, du, ds])
        else:
            summed = sum([from_sub[c, e, ds] for e in range(1, nsub)], marg[c, du, ds])
            if ds:
                from_sec.setdefault(c, []).append(shift(summed, "sec", nsec, ds))
                due.append(from_sec[c][-1])
            else:
                from_sec[c].insert(0, summed)
                running.append([c, 0])
                if (c, du, ds) == order[-1]:
                    due += boundary()

    nhalf = 2
    width = nfeat // nhalf
    totals = [jnp.zeros((ncol, width), jnp.float32)] * nhalf
    sketch_f = sketch_t.astype(jnp.float32)
    grads, parts, blocks, wide, lefts = [None] * nhalf, [None] * nhalf, [None] * nhalf, [None] * nhalf, [None] * nhalf

    def product(c, dus, half):
        names = [(c, du, ds) for du in dus for ds in range(nsec)]
        while any(name not in mixed for name in names):
            due.extend(boundary())
        mixes = [mixed[name] for name in names]
        mixes[0] = after(mixes[0], *older)
        totals[half] = back(mixes, [data[name] for name in names], totals[half], half)

    def close(half, *deps):
        total = totals[half] * SCALE
        cut = slice(half * width, (half + 1) * width)
        grads[half] = total[rank:] + LAM * own_weights[:, cut]
        parts[half] = total[:rank] + LAM * sketch_f[:, cut]
        lefts[half] = jnp.concatenate([LAM * sketch_f[:, cut] + parts[half], grads[half]], axis=0)
        blocks[half] = parts[half].astype(jnp.bfloat16)

    def send(half, ds, *deps):
        block = after(blocks[half], *deps)
        wide[half] = wide[half] or {0: blocks[half]}
        for d in ds:
            wide[half][d] = shift(block, "rows", nrows, -d)

    plan = [(0, [du], half) for half in range(nhalf) for du in range(nsub)]
    for c, dus, half in plan[:-1]:
        product(c, dus, half)
        older, due = due, boundary(totals[half])
    product(nchunk - 1, range(nsub), 0)
    close(0)
    direct = nrows <= 4
    if direct:
        send(0, range(1, nrows))
    c, dus, half = plan[-1]
    older = [totals[0]]
    product(c, dus, half)
    older = []
    for du in range(nsub):
        product(nchunk - 1, [du], 1)
        older = [wide[0][1]] if direct else []
    close(1)
    if direct:
        send(1, [1])

    prods = sum(
        lax.dot_general(left, part, (((1,), (1,)), ((), ())), precision=lax.Precision.HIGHEST)
        for left, part in zip(lefts, parts)
    )
    if direct:
        prods = after(prods, wide[0][1])
    prods = all_sum(prods, "sub", nsub)
    if direct:
        prods = after(prods, wide[0][nrows - 1])
    prods = all_sum(prods, "sec", nsec)
    if direct:
        prods = after(prods, *wide[0].values(), wide[1][1])
    prods = all_sum(prods, "rows", nrows)
    if direct:
        send(1, range(2, nrows), prods)
    step = solve(prods, jnp.concatenate(grads, axis=1), parts)

    def spread(x):
        parts = roll_to(collect(x, "rows", nrows, 0), 0, nrows, (nrows - z) % nrows)
        return jnp.moveaxis(parts, 0, 1).reshape(x.shape[0], -1).astype(jnp.float32)

    if direct:
        step = after(step, wide[1][nrows - 1])
    step = spread(step)[0]
    if direct:
        wide[1][0] = after(wide[1][0], step)
        out = None
        for half in range(nhalf):
            out = place(z, [wide[half][d] for d in range(nrows)], half, nhalf, out)
    else:
        out = spread(jnp.concatenate(blocks, axis=1))
    return (step, out.T)


def solution(mesh):
    placed = (
        P(("group", "rows")),
        P(("group", "rows")),
        P(("group", "sec", "sub")),
        P(("sec", "sub"), None),
    )
    sizes = tuple(mesh.shape[name] for name in ("rows", "sec", "sub"))
    return jax.shard_map(
        functools.partial(local, sizes),
        mesh=mesh,
        in_specs=placed,
        out_specs=(P(("group", "sec", "sub")), P(("group", "sec", "sub"), None)),
        check_vma=False,
    )
```

```python
import functools

import jax
import jax.numpy as jnp
from jax import lax
from jax.experimental import pallas as pl
from jax.experimental.pallas import tpu as pltpu
from jax.sharding import PartitionSpec as P

PRIME = 65521
FOLD = 46337
STEP_A = 30011
STEP_B = 16411
SHIFT = STEP_B * pow(STEP_A, -1, PRIME) % PRIME
LAM = 0.05
SCALE = 1.0 / 1024.0
LANES = 128
LEVEL = jnp.float8_e4m3fn


def window_table(length):
    rows = -(-length // (8 * LANES)) * 8
    n = lax.broadcasted_iota(jnp.int32, (rows, LANES), 0) * LANES + lax.broadcasted_iota(
        jnp.int32, (rows, LANES), 1
    )
    mixer = n % PRIME * STEP_A % PRIME
    folded = mixer % FOLD
    entry = (folded * folded % PRIME * 31 + 7) % PRIME
    return entry.astype(jnp.float32) - (PRIME - 0.5)


def window_starts(seeds, first):
    high = seeds * (SHIFT // 256) % PRIME
    return (high * 256 + seeds * (SHIFT % 256) + first) % PRIME


def whole_vmem():
    return pl.BlockSpec(memory_space=pltpu.VMEM)


def table_body(start_ref, tab_ref, a_ref, feat_ref, data_ref, marg_ref, scr, wide, *, unroll, pitch):
    nrow, nfeat = wide.shape
    nsub = nfeat // LANES
    high = min(8, nsub)
    lane = lax.broadcasted_iota(jnp.int32, (high, LANES), 1)
    base = pl.program_id(0) * nrow
    part = a_ref[...]

    def samples(group, carry):
        for u in range(unroll):
            row = group * unroll + u
            start = start_ref[base + row]
            top = start >> 7
            off = start & (LANES - 1)
            early = lane < off
            one = tab_ref[pl.ds(top, nsub), :]
            two = tab_ref[pl.ds(top + 1, nsub), :]
            for v in range(0, nsub, high):
                win = jnp.where(early, two[v : v + high], one[v : v + high])
                win = pltpu.roll(win, LANES - off, 1)
                level = (win + part[v : v + high]).astype(jnp.int32) & 15
                scr[pl.ds(row + v * pitch, high, stride=pitch), :] = level.astype(jnp.float32) - 7.5
        return carry

    lax.fori_loop(0, nrow // unroll, samples, 0)
    for r in range(nsub):
        cut = slice(r * LANES, (r + 1) * LANES)
        level = scr[pl.ds(r * pitch, nrow), :]
        wide[:, cut] = level.astype(jnp.bfloat16)
        data_ref[pl.ds(pl.multiple_of(base, nrow), nrow), cut] = level.astype(LEVEL)
    marg = lax.dot_general(
        wide[...], feat_ref[...], (((1,), (1,)), ((), ())), preferred_element_type=jnp.float32
    )
    marg_ref[...] = SCALE * marg.T[: marg_ref.shape[0]]


def make_table(starts, tab, part, feats, ncol):
    count = starts.shape[0]
    nsub = part.shape[0]
    nfeat = nsub * LANES
    nrow = min(256, count)
    pitch = nrow + 8
    return pl.pallas_call(
        functools.partial(table_body, unroll=min(128, nrow), pitch=pitch),
        grid_spec=pltpu.PrefetchScalarGridSpec(
            num_scalar_prefetch=1,
            grid=(count // nrow,),
            in_specs=[
                pl.BlockSpec(tab.shape, lambda i, s: (0, 0)),
                pl.BlockSpec(part.shape, lambda i, s: (0, 0)),
                pl.BlockSpec(feats.shape, lambda i, s: (0, 0)),
            ],
            out_specs=[
                whole_vmem(),
                pl.BlockSpec((ncol, nrow), lambda i, s: (0, i)),
            ],
            scratch_shapes=[
                pltpu.VMEM((nsub * pitch, LANES), jnp.float32),
                pltpu.VMEM((nrow, nfeat), jnp.bfloat16),
            ],
        ),
        out_shape=[
            pltpu.VMEM((count, nfeat), LEVEL),
            jax.ShapeDtypeStruct((ncol, count), jnp.float32),
        ],
        compiler_params=pltpu.CompilerParams(vmem_limit_bytes=12 << 20),
        cost_estimate=pl.CostEstimate(
            flops=count * nfeat * 1500, bytes_accessed=count * nfeat * 2, transcendentals=0
        ),
        name="make_table",
    )(starts, tab, part, feats)


def back_body(*refs, nblk, tile, half):
    mixes, datas, (old_ref, out_ref) = refs[:nblk], refs[nblk : 2 * nblk], refs[2 * nblk :]
    width = out_ref.shape[1]
    for at in range(0, width, tile):
        total = old_ref[:, at : at + tile]
        for mix_ref, data_ref in zip(mixes, datas):
            level = data_ref[:, half * width + at : half * width + at + tile].astype(jnp.bfloat16)
            total += jnp.dot(mix_ref[...], level, preferred_element_type=jnp.float32)
        out_ref[:, at : at + tile] = total


def back(mixes, datas, old, half):
    nblk = len(mixes)
    ncol, count = mixes[0].shape
    width = old.shape[1]
    return pl.pallas_call(
        functools.partial(back_body, nblk=nblk, tile=min(512, width), half=half),
        in_specs=[whole_vmem()] * (2 * nblk + 1),
        out_specs=whole_vmem(),
        out_shape=jax.ShapeDtypeStruct((ncol, width), jnp.float32),
        compiler_params=pltpu.CompilerParams(vmem_limit_bytes=12 << 20),
        cost_estimate=pl.CostEstimate(
            flops=2 * count * width * ncol * nblk, bytes_accessed=count * width * nblk, transcendentals=0
        ),
        name="back",
    )(*mixes, *datas, old)


def solve_body(prod_ref, grad_ref, *refs):
    step_ref = refs[-1]
    rank = prod_ref.shape[1]
    inner = prod_ref[:rank, :]
    mat = 0.5 * (inner + inner.T)
    rhs = prod_ref[rank : rank + 1, :]
    eye = (
        lax.broadcasted_iota(jnp.int32, (rank, rank), 0) == lax.broadcasted_iota(jnp.int32, (rank, rank), 1)
    ).astype(jnp.float32)
    col = jnp.sum(eye * rhs, axis=1, keepdims=True)
    row_of = lax.broadcasted_iota(jnp.int32, (rank, 1), 0)
    for k in range(rank):
        lead = mat[k : k + 1, :] / mat[k : k + 1, k : k + 1]
        head = col[k : k + 1, :] / mat[k : k + 1, k : k + 1]
        by = jnp.where(row_of == k, 0.0, mat[:, k : k + 1])
        mat = jnp.where(row_of == k, lead, mat - by * lead)
        col = jnp.where(row_of == k, head, col - by * head)
    at = 0
    for ref in refs[:-1]:
        width = ref.shape[1]
        fit = jnp.sum(ref[...] * col, axis=0, keepdims=True)
        step_ref[:, at : at + width] = (grad_ref[:, at : at + width] - fit) * (1.0 / LAM)
        at += width


def solve(prods, grad, halves):
    return pl.pallas_call(
        solve_body,
        out_shape=jax.ShapeDtypeStruct(grad.shape, jnp.float32),
        compiler_params=pltpu.CompilerParams(vmem_limit_bytes=8 << 20),
        name="solve",
    )(prods, grad, *halves)


def place_body(at_ref, *refs, size):
    for d in range(size):

        @pl.when(pl.program_id(0) == d)
        def _():
            refs[-1][...] = refs[d][...].astype(jnp.float32)


def place(z, parts, half, nhalf, old=None):
    size = len(parts)
    rank, width = parts[0].shape
    extra = [] if old is None else [old]
    return pl.pallas_call(
        functools.partial(place_body, size=size),
        grid_spec=pltpu.PrefetchScalarGridSpec(
            num_scalar_prefetch=1,
            grid=(size,),
            in_specs=[pl.BlockSpec((rank, width), lambda d, at: (0, 0))] * size
            + [pl.BlockSpec(memory_space=pl.ANY)] * len(extra),
            out_specs=pl.BlockSpec((rank, width), lambda d, at: (0, lax.rem(at[0] + d, size) * nhalf + half)),
        ),
        out_shape=jax.ShapeDtypeStruct((rank, width * nhalf * size), jnp.float32),
        input_output_aliases={1 + size: 0} if extra else {},
        compiler_params=pltpu.CompilerParams(vmem_limit_bytes=8 << 20),
        name="place",
    )(z.reshape(1), *parts, *extra)


def shift(x, axis, size, by):
    return lax.ppermute(x, axis, [(i, (i + by) % size) for i in range(size)])


def scatter_sum(x, axis, size):
    if size <= 4:
        total = x[:, 0]
        for d in range(1, size):
            total = total + shift(x[:, d], axis, size, d)
        return total

    def hop(i, acc):
        return shift(acc, axis, size, 1) + lax.dynamic_index_in_dim(x, size - 2 - i, 1, False)

    return lax.fori_loop(0, size - 1, hop, x[:, size - 1])


def collect(x, axis, size, at):
    if size <= 4:
        return jnp.stack([x] + [shift(x, axis, size, -d) for d in range(1, size)], axis=at)

    def hop(cur, _):
        cur = shift(cur, axis, size, -1)
        return cur, cur

    _, rest = lax.scan(hop, x, None, length=size - 1)
    return jnp.moveaxis(jnp.concatenate([x[None], rest], axis=0), 0, at)


def all_sum(x, axis, size):
    if size == 2:
        return x + shift(x, axis, size, 1)
    if size == 4:
        one, two, three = (shift(x, axis, size, -d) for d in (1, 2, 3))
        even = lax.axis_index(axis) % 2 == 0
        return (x + jnp.where(even, one, three)) + (two + jnp.where(even, three, one))
    return lax.psum(x, axis)


def roll_to(x, dim, size, index):
    return lax.dynamic_slice_in_dim(jnp.concatenate([x, x], axis=dim), index, size, dim)


def weigh(margins, labels):
    prob = jax.nn.sigmoid(margins[-1:])
    resid = prob - labels.astype(jnp.float32)
    return jnp.concatenate([prob * (1.0 - prob) * margins[:-1], resid], axis=0).astype(jnp.bfloat16)


def after(x, *deps):
    return lax.optimization_barrier((x, *deps))[0]


def split(x, size, at):
    width = x.shape[1] // size
    return x[:, at * width : (at + 1) * width]


def scatter_rows(x, size):
    if size <= 4:
        return split(x, size, 0), [shift(split(x, size, d), "rows", size, d) for d in range(1, size)]
    return scatter_sum(x.reshape(x.shape[0], size, -1), "rows", size), []


def collect_rows(x, size):
    if size <= 4:
        return [x] + [shift(x, "rows", size, -d) for d in range(1, size)]
    return [collect(x, "rows", size, 1).reshape(x.shape[0], -1)]


def local(sizes, row_seeds, labels, weights, sketch):
    nrows, nsec, nsub = sizes
    count = row_seeds.shape[0]
    rank = sketch.shape[1]
    nfeat = weights.shape[0] // nrows
    z, s, u = lax.axis_index("rows"), lax.axis_index("sec"), lax.axis_index("sub")
    own = z * nfeat
    first = (s * nsub + u) * weights.shape[0] + own

    nchunk = 2
    piece = count // (nchunk * nsec * nsub)
    seeds = row_seeds.reshape(nchunk, nsec, nsub, piece)
    seeds = roll_to(roll_to(seeds, 1, nsec, s), 2, nsub, u)
    starts = window_starts(collect(seeds, "rows", nrows, 3), first)
    labels = labels.reshape(nchunk, nsec, nsub, piece)
    labels = lax.dynamic_slice(labels, (0, s, u, 0), (nchunk, 1, 1, piece)).reshape(nchunk, 1, piece)

    tab = window_table(PRIME + nfeat + LANES)
    cols = first + lax.iota(jnp.int32, nfeat)
    part = (cols * STEP_A % PRIME).astype(jnp.float32).reshape(nfeat // LANES, LANES)
    sketch_t = lax.dynamic_slice_in_dim(sketch.T, own, nfeat, 1)
    own_weights = lax.dynamic_slice_in_dim(weights, own, nfeat, 0)[None]
    feats = jnp.concatenate([sketch_t, own_weights.astype(jnp.bfloat16)], axis=0)
    ncol = rank + 1
    padded = jnp.pad(feats, ((0, -ncol % LANES), (0, 0)))

    order = [(c, du, ds) for c in range(nchunk) for du in reversed(range(nsub)) for ds in reversed(range(nsec))]
    data, marg, from_sub, from_sec, mixed, stage = {}, {}, {}, {}, {}, {}
    older, due = [], []

    def advance(c, at, *deps):
        if at == 0:
            held, come = scatter_rows(sum(from_sec[c][1:], from_sec[c][0]), nrows)
            stage[c] = (held, come)
            return come or [held]
        if at == 1:
            held, come = stage[c]
            held = after(held, *deps)
            come = [after(x, *deps) for x in come]
            stage[c] = collect_rows(weigh(sum(come, held), labels[c]), nrows)
            return stage[c]
        if at == 2:
            mixed[c, 0, 0] = jnp.concatenate([after(x, *deps) for x in stage[c]], axis=1)
            for ds in range(1, nsec):
                mixed[c, 0, ds] = shift(mixed[c, 0, 0], "sec", nsec, -ds)
            return [mixed[c, 0, ds] for ds in range(1, nsec)]
        if at == 3:
            half = jnp.concatenate([after(mixed[c, 0, ds], *deps) for ds in range(nsec)], axis=1)
            for du in range(1, nsub):
                come = shift(half, "sub", nsub, -du)
                for ds in range(nsec):
                    mixed[c, du, ds] = split(come, nsec, ds)
            return [mixed[c, nsub - 1, 0]]
        return []

    running = []

    def boundary(*deps):
        out = []
        for chunk in list(running):
            out += advance(chunk[0], chunk[1], *deps)
            chunk[1] += 1
            if chunk[1] > 3:
                running.remove(chunk)
        return out

    last = []
    for c, du, ds in order:
        begin = after(starts[c, ds, du].reshape(-1), *last, *older)
        data[c, du, ds], marg[c, du, ds] = make_table(begin, tab, part, padded, ncol)
        last = [marg[c, du, ds]]
        older, due = due, boundary(*last)
        if du:
            from_sub[c, du, ds] = shift(marg[c, du, ds], "sub", nsub, du)
            due.append(from_sub[c, du, ds])
        else:
            summed = sum([from_sub[c, e, ds] for e in range(1, nsub)], marg[c, du, ds])
            if ds:
                from_sec.setdefault(c, []).append(shift(summed, "sec", nsec, ds))
                due.append(from_sec[c][-1])
            else:
                from_sec[c].insert(0, summed)
                running.append([c, 0])
                if (c, du, ds) == order[-1]:
                    due += boundary()

    nhalf = 2
    width = nfeat // nhalf
    totals = [jnp.zeros((ncol, width), jnp.float32)] * nhalf
    sketch_f = sketch_t.astype(jnp.float32)
    grads, parts, blocks, wide, lefts = [None] * nhalf, [None] * nhalf, [None] * nhalf, [None] * nhalf, [None] * nhalf

    def product(c, dus, half):
        names = [(c, du, ds) for du in dus for ds in range(nsec)]
        while any(name not in mixed for name in names):
            due.extend(boundary())
        mixes = [mixed[name] for name in names]
        mixes[0] = after(mixes[0], *older)
        totals[half] = back(mixes, [data[name] for name in names], totals[half], half)

    def close(half, *deps):
        total = totals[half] * SCALE
        cut = slice(half * width, (half + 1) * width)
        grads[half] = total[rank:] + LAM * own_weights[:, cut]
        parts[half] = total[:rank] + LAM * sketch_f[:, cut]
        lefts[half] = jnp.concatenate([LAM * sketch_f[:, cut] + parts[half], grads[half]], axis=0)
        blocks[half] = parts[half].astype(jnp.bfloat16)

    def send(half, ds, *deps):
        block = after(blocks[half], *deps)
        wide[half] = wide[half] or {0: blocks[half]}
        for d in ds:
            wide[half][d] = shift(block, "rows", nrows, -d)

    plan = [(0, [du], half) for half in range(nhalf) for du in range(nsub)]
    for c, dus, half in plan[:-1]:
        product(c, dus, half)
        older, due = due, boundary(totals[half])
    product(nchunk - 1, range(nsub), 0)
    close(0)
    direct = nrows <= 4
    if direct:
        send(0, range(1, nrows))
    c, dus, half = plan[-1]
    older = [totals[0]]
    product(c, dus, half)
    older = []
    for du in range(nsub):
        product(nchunk - 1, [du], 1)
        older = [wide[0][1]] if direct else []
    close(1)
    if direct:
        send(1, [1])

    prods = sum(
        lax.dot_general(left, part, (((1,), (1,)), ((), ())), precision=lax.Precision.HIGHEST)
        for left, part in zip(lefts, parts)
    )
    if direct:
        prods = after(prods, wide[0][1])
    prods = all_sum(prods, "sub", nsub)
    if direct:
        prods = after(prods, wide[0][nrows - 1])
    prods = all_sum(prods, "sec", nsec)
    if direct:
        prods = after(prods, *wide[0].values(), wide[1][1])
    prods = all_sum(prods, "rows", nrows)
    if direct:
        send(1, range(2, nrows), prods)
    step = solve(prods, jnp.concatenate(grads, axis=1), parts)

    def spread(x):
        parts = roll_to(collect(x, "rows", nrows, 0), 0, nrows, (nrows - z) % nrows)
        return jnp.moveaxis(parts, 0, 1).reshape(x.shape[0], -1).astype(jnp.float32)

    if direct:
        wide[1][0] = after(wide[1][0], step)
        step = after(step, wide[1][nrows - 1])
    step = spread(step)[0]
    if direct:
        out = None
        for half in range(nhalf):
            out = place(z, [wide[half][d] for d in range(nrows)], half, nhalf, out)
    else:
        out = spread(jnp.concatenate(blocks, axis=1))
    return (step, out.T)


def solution(mesh):
    placed = (
        P(("group", "rows")),
        P(("group", "rows")),
        P(("group", "sec", "sub")),
        P(("sec", "sub"), None),
    )
    sizes = tuple(mesh.shape[name] for name in ("rows", "sec", "sub"))
    return jax.shard_map(
        functools.partial(local, sizes),
        mesh=mesh,
        in_specs=placed,
        out_specs=(P(("group", "sec", "sub")), P(("group", "sec", "sub"), None)),
        check_vma=False,
    )
```
